32 devices in a mesh: doc: 8 (over z, x), bkt: 4 (over y, core).
Axes of the slice: x: 2, y: 2, z: 4, core: 2. Of those that a mesh axis runs over, the one named last changes fastest.
Arguments:
- start_vectors: float32 [64, 32768], P(None, ('doc', 'bkt')), may hold values from -6 to 6
- bucket_weight: float32 [8192], P('bkt'), may hold values from 0.1 to 1
- tile_count: int32 [8, 4], P('doc', 'bkt'), may hold values from 128 to 256, as said below
- tile_coords: int32 [8, 4, 256, 2], P('doc', 'bkt'), may hold values from 0 to 31, as said below
- patterns: int32 [8, 4, 256, 128, 128], P('doc', 'bkt'), may hold values from 0 to 1
Outputs:
- eigen_block: float32 [64, 32768], P(None, ('doc', 'bkt'))
The draws below stay inside these ranges and needn't reach their ends.
Inputs may be any that keep to these rules, and one draw needn't show every extreme that they name: `tile_count`: the largest count is exactly 256 in every draw. `tile_coords`: row tiles lie below 32, column tiles below 16; the pairs of one document band and bucket band are distinct.
All inputs are finite; a program needn't handle non-finite values.
Results may differ from the reference program's by a relative error of at most 0.018.
Values may be sent and summed in bfloat16 or wider, within the bound.
A program may use at most 128 MiB of HBM per device.

```python
import math
import jax
import jax.numpy as jnp
from jax import lax

K = 64
TILE = 128
ITERS = 2
DOC_BAND = 4096
TMAX = 256
DOC_BANDS = 8
BKT_BANDS = 4
BKT_BAND = 2048
NDOC = 32768
NBKT = 8192


def draw_tile_count(key, part):
    device_total = DOC_BANDS * BKT_BANDS
    base = jax.random.randint(jax.random.fold_in(key, 21), (device_total,), TMAX // 2, TMAX + 1)
    fullest = jax.random.randint(jax.random.fold_in(key, 22), (), 0, device_total)
    counts = jnp.where(jnp.arange(device_total) == fullest, TMAX, base)
    return counts.reshape(DOC_BANDS, BKT_BANDS).astype(jnp.int32)


def draw_tile_coords(key, part):
    row_tiles = DOC_BAND // TILE
    col_tiles = BKT_BAND // TILE
    keys = jax.random.split(jax.random.fold_in(key, 11), DOC_BANDS * BKT_BANDS)
    picks = jax.vmap(lambda single: jax.random.permutation(single, row_tiles * col_tiles)[:TMAX])(keys)
    coords = jnp.stack([picks // col_tiles, picks % col_tiles], axis=-1)
    return coords.reshape(DOC_BANDS, BKT_BANDS, TMAX, 2).astype(jnp.int32)


def draw_patterns(key, part):
    shape_rows = (DOC_BANDS, BKT_BANDS, TMAX, TILE, 1)
    shape_full = (DOC_BANDS, BKT_BANDS, TMAX, TILE, TILE)
    levels = jax.random.randint(jax.random.fold_in(key, 31), shape_rows, 1, 17)
    values = jax.random.randint(jax.random.fold_in(key, 32), shape_full, 0, 256)
    return (values < levels).astype(jnp.int32)


def shard_levels(key, dims, shards, low, largest):
    level = 1.0
    for axis_at, blocks in shards:
        draws = jax.random.uniform(jax.random.fold_in(jax.random.fold_in(key, 6), axis_at), (blocks,), jnp.float32, low / len(shards), largest / len(shards))
        level = level * jnp.repeat(jnp.exp(draws), dims[axis_at] // blocks).reshape((-1,) + (1,) * (len(dims) - 1 - axis_at))
    return level


def gaussian(key, extent, width, reach, cuts=(), kind=jnp.bfloat16):
    drawn = width * jax.random.normal(key, extent, jnp.float32)
    if cuts:
        drawn = drawn * shard_levels(key, extent, cuts, -0.22, 0.18)
    return jnp.clip(drawn, -reach, reach).astype(kind)


def setup_inputs(seed: int = 0) -> dict:
    key_list = jax.random.split(jax.random.key(seed), 6)
    start_vectors = gaussian(key_list[0], (K, NDOC), 1.0, 6.0, ((1, 32),), jnp.float32)
    bucket_weight = jnp.clip(jnp.exp(math.log(1.0) - 2.3025851 * jax.random.uniform(key_list[1], (NBKT,), jnp.float32) ** shard_levels(key_list[1], (NBKT,), ((0, 4),), -0.2, 0.2)), 0.1, 1.0)
    tile_count = draw_tile_count(jax.random.fold_in(key_list[5], 71), 0)
    tile_coords = draw_tile_coords(jax.random.fold_in(key_list[5], 71), 0)
    patterns = draw_patterns(jax.random.fold_in(key_list[5], 71), 0)
    return dict(start_vectors=start_vectors, bucket_weight=bucket_weight, tile_count=tile_count, tile_coords=tile_coords, patterns=patterns)


def reference(start_vectors, bucket_weight, tile_count, tile_coords, patterns):
    row_tiles = DOC_BAND // TILE
    col_tiles = BKT_BAND // TILE
    device_total = DOC_BANDS * BKT_BANDS
    band_doc = jnp.repeat(jnp.arange(DOC_BANDS, dtype=jnp.int32), BKT_BANDS)
    band_bkt = jnp.tile(jnp.arange(BKT_BANDS, dtype=jnp.int32), DOC_BANDS)
    coords = tile_coords.reshape(device_total, TMAX, 2)
    global_rows = (band_doc[:, None] * row_tiles + coords[:, :, 0]).astype(jnp.int32)
    global_cols = (band_bkt[:, None] * col_tiles + coords[:, :, 1]).astype(jnp.int32)
    live_slot = jnp.arange(TMAX, dtype=jnp.int32)[None, :] < tile_count.reshape(device_total)[:, None]
    tiles_all = patterns.reshape(device_total, TMAX, TILE, TILE)
    items = (tiles_all, global_rows, global_cols, live_slot)
    weight_tiles = bucket_weight.reshape(NBKT // TILE, TILE)

    def masked_tiles(tiles, live):
        return jnp.where(live[:, None, None], tiles, 0).astype(jnp.float32)

    def degree_step(carry, item):
        doc_sum, bucket_sum = carry
        tiles, rows, cols, live = item
        masked = masked_tiles(tiles, live)
        row_part = jnp.einsum('tij,tj->ti', masked, weight_tiles[cols], precision=lax.Precision.HIGHEST)
        doc_sum = doc_sum.at[rows].add(row_part)
        bucket_sum = bucket_sum.at[cols].add(lax.optimization_barrier(jnp.sum(masked, axis=1)))
        return ((doc_sum, bucket_sum), None)
    start = (jnp.zeros((NDOC // TILE, TILE), jnp.float32), jnp.zeros((NBKT // TILE, TILE), jnp.float32))
    (doc_sum, bucket_sum), _ = lax.scan(degree_step, start, items)
    inv_doc = 1.0 / jnp.sqrt(jnp.maximum(doc_sum.reshape(NDOC), 1.0))
    bucket_scale = bucket_weight / jnp.maximum(bucket_sum.reshape(NBKT), 1.0)
    block = start_vectors
    for sweep_index in range(ITERS):
        scaled = (block * inv_doc[None, :]).astype(jnp.bfloat16)
        scaled_tiles = scaled.reshape(K, NDOC // TILE, TILE)

        def forward_step(carry, item):
            tiles, rows, cols, live = item
            masked = masked_tiles(tiles, live)
            picked = scaled_tiles[:, rows, :].astype(jnp.float32)
            terms = jnp.einsum('kti,tij->ktj', picked, masked, precision=lax.Precision.HIGHEST)
            return (carry.at[:, cols, :].add(terms), None)
        panel, _ = lax.scan(forward_step, jnp.zeros((K, NBKT // TILE, TILE), jnp.float32), items)
        weighted = (panel.reshape(K, NBKT) * bucket_scale[None, :]).astype(jnp.bfloat16)
        weighted_tiles = weighted.reshape(K, NBKT // TILE, TILE)

        def backward_step(carry, item):
            tiles, rows, cols, live = item
            masked = masked_tiles(tiles, live)
            picked = weighted_tiles[:, cols, :].astype(jnp.float32)
            terms = jnp.einsum('ktj,tij->kti', picked, masked, precision=lax.Precision.HIGHEST)
            return (carry.at[:, rows, :].add(terms), None)
        image, _ = lax.scan(backward_step, jnp.zeros((K, NDOC // TILE, TILE), jnp.float32), items)
        image = image.reshape(K, NDOC) * inv_doc[None, :]
        gram_matrix = jnp.dot(image, image.T, precision=lax.Precision.HIGHEST) / NDOC
        factor = jnp.linalg.cholesky(gram_matrix)
        block = lax.linalg.triangular_solve(factor, image, left_side=True, lower=True)
    return block
```

```python
import functools
import types

import jax
import jax.numpy as jnp
from jax import lax
from jax.experimental import pallas as pl
from jax.experimental.pallas import tpu as pltpu
from jax.sharding import PartitionSpec as P

ITERS = 2


def plain_body(start_vectors, bucket_weight, tile_count, tile_coords, patterns):
    highest = lax.Precision.HIGHEST
    slot_total = patterns.shape[2]
    tile_size = patterns.shape[3]
    vector_count = start_vectors.shape[0]
    own_rows = start_vectors.shape[1]
    band_rows = own_rows * lax.axis_size("bkt")
    band_cols = bucket_weight.shape[0]
    row_tiles = band_rows // tile_size
    col_tiles = band_cols // tile_size
    total_docs = band_rows * lax.axis_size("doc")
    live_slot = (jnp.arange(slot_total) < tile_count[0, 0]).astype(jnp.int32)
    pattern_int = patterns[0, 0] * live_slot[:, None, None]
    pattern = pattern_int.astype(jnp.bfloat16)
    row_index = tile_coords[0, 0, :, 0]
    col_index = tile_coords[0, 0, :, 1]
    row_pick = jnp.arange(row_tiles)[:, None] == row_index[None, :]
    col_pick = jnp.arange(col_tiles)[:, None] == col_index[None, :]
    row_pick_f = row_pick.astype(jnp.float32)
    row_pick_b = row_pick.astype(jnp.bfloat16)
    col_pick_f = col_pick.astype(jnp.float32)
    col_pick_b = col_pick.astype(jnp.bfloat16)
    pattern_f = pattern_int.astype(jnp.float32)
    weight_tiles = bucket_weight.reshape(col_tiles, tile_size)
    slot_weight = jnp.dot(col_pick_f.T, weight_tiles, precision=highest)
    row_part = jnp.einsum("tij,tj->ti", pattern_f, slot_weight, precision=highest)
    doc_part = jnp.dot(row_pick_f, row_part, precision=highest).reshape(band_rows)
    col_part = jnp.sum(pattern_f, axis=1)
    bucket_part = jnp.dot(col_pick_f, col_part, precision=highest).reshape(band_cols)
    doc_degree = lax.psum(doc_part, "bkt")
    bucket_size = lax.psum(bucket_part.astype(jnp.bfloat16), "doc").astype(jnp.float32)
    inv_band = 1.0 / jnp.sqrt(jnp.maximum(doc_degree, 1.0))
    inv_own = lax.dynamic_slice_in_dim(inv_band, lax.axis_index("bkt") * own_rows, own_rows)
    bucket_scale = bucket_weight / jnp.maximum(bucket_size, 1.0)
    vectors = start_vectors
    for sweep_index in range(ITERS):
        scaled = (vectors * inv_own[None, :]).astype(jnp.bfloat16)
        band_vecs = lax.all_gather(scaled, "bkt", axis=1, tiled=True)
        picked = jnp.einsum(
            "rt,kri->kti",
            row_pick_b,
            band_vecs.reshape(vector_count, row_tiles, tile_size),
            preferred_element_type=jnp.float32,
        ).astype(jnp.bfloat16)
        products = jnp.einsum("kti,tij->ktj", picked, pattern, preferred_element_type=jnp.float32)
        panel_part = (
            jnp.zeros((vector_count, col_tiles, tile_size), jnp.float32)
            .at[:, col_index, :]
            .add(products)
        )
        panel_part = panel_part.reshape(vector_count, band_cols)
        panel_whole = lax.psum(panel_part, "doc")
        weighted = (panel_whole * bucket_scale[None, :]).astype(jnp.bfloat16)
        spread = jnp.einsum(
            "ct,kcj->ktj",
            col_pick_b,
            weighted.reshape(vector_count, col_tiles, tile_size),
            preferred_element_type=jnp.float32,
        ).astype(jnp.bfloat16)
        returned = jnp.einsum("ktj,tij->kti", spread, pattern, preferred_element_type=jnp.float32)
        row_terms = (
            jnp.zeros((vector_count, row_tiles, tile_size), jnp.float32)
            .at[:, row_index, :]
            .add(returned)
        )
        row_terms = row_terms.reshape(vector_count, band_rows)
        rows_own = (
            lax.psum_scatter(row_terms, "bkt", scatter_dimension=1, tiled=True) * inv_own[None, :]
        )
        gram_local = jnp.dot(rows_own, rows_own.T, precision=highest)
        gram_matrix = lax.psum(gram_local, ("doc", "bkt")) / total_docs
        factor = jnp.linalg.cholesky(gram_matrix)
        vectors = lax.linalg.triangular_solve(factor, rows_own, left_side=True, lower=True)
    return vectors


MESH = pl.DeviceIdType.MESH
F32 = jnp.float32
BF16 = jnp.bfloat16
I32 = jnp.int32
NT = (((1,), (1,)), ((), ()))
BLOCK = 4
CHUNKS = 8
GROUP = 16


def flip(value, k, bits):
    out = 0
    for at in range(bits):
        unit = 1 << at
        bit = lax.rem(lax.div(value, unit), 2)
        want = (k >> at) & 1 if isinstance(k, int) else lax.rem(lax.div(k, unit), 2)
        out = out + unit * (bit + want - 2 * bit * want)
    return out


def inverse_factor(gram, k_vec):
    row_at = lax.broadcasted_iota(I32, (k_vec, k_vec), 0)
    col_at = lax.broadcasted_iota(I32, (k_vec, k_vec), 1)
    eye = (row_at == col_at).astype(F32)
    work = jnp.concatenate([gram, eye], axis=1)
    for at in range(0, k_vec, BLOCK):
        top = at // 8 * 8
        part = work[top:]
        below = lax.broadcasted_iota(I32, part.shape, 0)
        cols = [jnp.broadcast_to(part[:, at + m : at + m + 1], part.shape) for m in range(BLOCK)]
        for m in range(BLOCK):
            row = at - top + m
            factor = jnp.where(below > row, cols[m] * (1.0 / cols[m][row : row + 1]), 0.0)
            part = part - factor * part[row : row + 1]
            for n in range(m + 1, BLOCK):
                cols[n] = cols[n] - factor * cols[n][row : row + 1]
        work = jnp.concatenate([work[:top], part], axis=0) if top else part
    pivots = jnp.sum(work[:, :k_vec] * eye, axis=1, keepdims=True)
    return work[:, k_vec:] / jnp.sqrt(pivots)


def kernel(names, nd, nb, count_ref, coord_ref, place_ref, start_hbm, weight_hbm, patterns_hbm, out_ref, *refs):
    s = types.SimpleNamespace(**dict(zip(names, refs, strict=True)))
    highest = lax.Precision.HIGHEST
    me_d = lax.axis_index("doc")
    me_b = lax.axis_index("bkt")
    d_bits, b_bits = nd.bit_length() - 1, nb.bit_length() - 1
    slots, tile = patterns_hbm.shape[0], patterns_hbm.shape[1]
    k_vec, own_rows = s.start.shape
    col_tiles = s.weight.shape[0]
    col_per = col_tiles // nd
    row_per = own_rows // tile
    own_cols = col_per * tile
    total_docs = own_rows * nb * nd
    nz = nd // 2

    def to(kd, kb):
        return {"doc": flip(me_d, kd, d_bits), "bkt": flip(me_b, kb, b_bits)}

    def remote(src, dst, ssem, rsem, peer):
        return pltpu.make_async_remote_copy(
            src_ref=src, dst_ref=dst, send_sem=ssem, recv_sem=rsem,
            device_id=peer, device_id_type=MESH,
        )

    def send(*args):
        copy = remote(*args)
        copy.start()
        return copy

    load_start = pltpu.make_async_copy(start_hbm, s.start, s.small_sem.at[0])
    load_start.start()
    load_weight = pltpu.make_async_copy(weight_hbm, s.weight, s.small_sem.at[1])
    load_weight.start()
    per_chunk = slots // CHUNKS

    def load(c):
        part = pl.ds(c * per_chunk, per_chunk)
        return pltpu.make_async_copy(patterns_hbm.at[part], s.tiles.at[part], s.load_sem.at[c])

    for c in range(CHUNKS):
        load(c).start()

    barrier = pltpu.get_barrier_semaphore()
    peers = [(kd, kb) for kd in range(nd) for kb in range(nb) if (kd < 2 or kb == 0) and kd + kb]
    for kd, kb in peers:
        pl.semaphore_signal(barrier, inc=1, device_id=to(kd, kb), device_id_type=MESH)

    lane = lax.broadcasted_iota(I32, (1, slots), 1)
    place = place_ref[0:1, :] * col_tiles + place_ref[1:2, :]
    place = jnp.where(lane < count_ref[0, 0], place, -1)
    across = jnp.transpose(jnp.broadcast_to(place, (tile, slots)))
    position = lax.broadcasted_iota(I32, (slots, tile), 1)
    slot_at = lax.broadcasted_iota(I32, (slots, tile), 0)
    for b in range(nb):
        found = jnp.max(jnp.where(across == position + b * tile, slot_at, -1), axis=0, keepdims=True)
        s.table[b : b + 1, :] = jnp.where(found >= 0, found, slots)
    tables = pltpu.make_async_copy(s.table, s.slot, s.small_sem.at[2])
    tables.start()
    s.bits[slots] = jnp.zeros((tile, tile), BF16)
    s.size_terms[slots] = jnp.zeros((8, tile), F32)
    s.doc_terms[slots] = jnp.zeros((8, tile), F32)

    load_weight.wait()
    for c in range(col_tiles):
        left = s.weight[c : c + 1, :]
        terms = []
        for _ in range(3):
            terms.append(left.astype(BF16).astype(F32))
            left = left - terms[-1]
        zeros = jnp.zeros((5, tile), F32)
        gap = jnp.zeros((8, tile), F32)
        eight = jnp.concatenate(terms + [zeros], axis=0)
        s.weight_terms[0, c] = jnp.concatenate([eight, gap], axis=0).astype(BF16)
        s.weight_terms[1, c] = jnp.concatenate([gap, eight], axis=0).astype(BF16)
    load_start.wait()
    s.raw[0] = s.start[...].astype(BF16)
    pl.semaphore_wait(barrier, len(peers))

    def gather_start(buf, ssem, rsem):
        return [
            send(buf.at[0], buf.at[k], ssem.at[k], rsem.at[k], to(0, k))
            for k in (2, 1)
        ]

    def gather_relay(buf, ssem, rsem, sent):
        sent[0].wait_recv()
        sent.append(send(buf.at[2], buf.at[3], ssem.at[3], rsem.at[3], to(0, 1)))

    waits = gather_start(s.raw, s.raw_send, s.raw_recv)
    raw_sent = waits


    @pl.loop(0, CHUNKS)
    def _(c):
        load(c).wait()

        @pl.loop(0, per_chunk // GROUP)
        def _(g):
            base = c * per_chunk + g * GROUP
            for u in range(0, GROUP, 2):
                pair = []
                for v in range(2):
                    at = base + u + v
                    block = s.tiles[at].astype(F32)
                    s.size_terms[at] = jnp.sum(block.reshape(tile // 8, 8, tile), axis=0)
                    pair.append(block.astype(BF16))
                    s.bits[at] = pair[v]
                left = jnp.concatenate(
                    [s.weight_terms[0, coord_ref[1, base + u]], s.weight_terms[1, coord_ref[1, base + u + 1]]], axis=1
                )
                sums = lax.dot_general(left, jnp.concatenate(pair, axis=1), NT, preferred_element_type=F32)
                s.doc_terms[base + u] = sums[:8]
                s.doc_terms[base + u + 1] = sums[8:]

    tables.wait()
    gather_relay(s.raw, s.raw_send, s.raw_recv, raw_sent)

    def slot_of(b, i, c):
        return s.slot[b, i * col_tiles + c]

    for b in range(nb):
        for i in range(row_per):
            total = s.doc_terms[slot_of(b, i, 0)]
            for c in range(1, col_tiles):
                total = total + s.doc_terms[slot_of(b, i, c)]
            s.degree_own[b * row_per + i : b * row_per + i + 1, :] = total[0:1] + total[1:2] + total[2:3]
    s.degree[me_b] = s.degree_own[...]
    degree_sent = [
        send(s.degree.at[me_b], s.degree.at[me_b], s.deg_send.at[k], s.deg_recv.at[k], to(0, k))
        for k in range(nb - 1, 0, -1)
    ]
    for c in range(col_tiles):
        total = s.size_terms[slot_of(0, 0, c)]
        for b in range(nb):
            for i in range(0 if b else 1, row_per):
                total = total + s.size_terms[slot_of(b, i, c)]
        total = jnp.sum(total, axis=0, keepdims=True)
        s.size[c // col_per, :, c % col_per * tile : (c % col_per + 1) * tile] = total
    size_sent = []
    for k in range(nd - 1, 0, -1):
        size_sent.append(
            send(s.size.at[flip(me_d, k, d_bits)], s.size_from.at[k], s.size_send.at[k], s.size_recv.at[k], to(k, 0))
        )
    for copy in degree_sent:
        copy.wait()
    degree = s.degree[0]
    for b in range(1, nb):
        degree = degree + s.degree[b]
    s.inv[...] = 1.0 / jnp.sqrt(jnp.maximum(degree, 1.0))
    for copy in raw_sent[1:]:
        copy.wait_recv()
    for k in range(nb):
        first = flip(me_b, k, b_bits) * row_per
        inv_rows = s.inv[pl.ds(pl.multiple_of(first, row_per), row_per), :]
        for i in range(row_per):
            lanes = slice(i * tile, (i + 1) * tile)
            s.band[0, k, :, lanes] = (s.raw[k, :, lanes].astype(F32) * inv_rows[i : i + 1]).astype(BF16)
    inv_own = s.inv[pl.ds(pl.multiple_of(me_b * row_per, row_per), row_per), :]

    def tiles_of(b, i, o):
        pick = [[s.bits[slot_of(b, i + u, o * col_per + h)] for h in range(col_per)] for u in range(2)]
        return jnp.concatenate([jnp.concatenate(row, axis=1) for row in pick], axis=0)

    def panel_of(it, kd, sources, acc):
        o = flip(me_d, kd, d_bits)
        for k in sources:
            b = flip(me_b, k, b_bits)
            for i in range(0, row_per, 2):
                left = s.band[it, k, :, i * tile : (i + 2) * tile]
                term = jnp.dot(left, tiles_of(b, i, o), preferred_element_type=F32)
                acc = term if acc is None else acc + term
        return acc

    def image_of(q, left, o):
        right = jnp.concatenate([tiles_of(q, i, o) for i in range(0, row_per, 2)], axis=0)
        return lax.dot_general(left, right, NT, preferred_element_type=F32)

    def gram_start(it, image):
        high = image.astype(BF16)
        low = (image - high.astype(F32)).astype(BF16)
        both = jnp.concatenate([high, low], axis=0)
        gram = lax.dot_general(both, both, NT, preferred_element_type=F32)
        gram = gram[:k_vec] + gram[k_vec:]
        gram = gram[:, :k_vec] + gram[:, k_vec:]
        half = k_vec // 2
        mine = lax.rem(me_d, 2) * nb + me_b
        s.gram_one[it, mine] = jnp.concatenate([gram[:half], gram[half:]], axis=1)
        return [
            send(s.gram_one.at[it, mine], s.gram_one.at[it, mine], s.g1_send.at[it, k], s.g1_recv.at[it, k], to(k // nb, k % nb))
            for k in range(2 * nb - 1, 0, -1)
        ]

    def gram_middle(it, sent):
        for copy in sent:
            copy.wait_recv()
        total = s.gram_one[it, 0]
        for k in range(1, 2 * nb):
            total = total + s.gram_one[it, k]
        mine = lax.div(me_d, 2)
        s.gram_two[it, mine] = total
        return [
            send(s.gram_two.at[it, mine], s.gram_two.at[it, mine], s.g2_send.at[it, k], s.g2_recv.at[it, k], to(2 * k, 0))
            for k in range(nz - 1, 0, -1)
        ]

    def gram_end(it, sent):
        for copy in sent:
            copy.wait_recv()
        total = s.gram_two[it, 0]
        for k in range(1, nz):
            total = total + s.gram_two[it, k]
        return jnp.concatenate([total[:, :k_vec], total[:, k_vec:]], axis=0) / total_docs

    waits = list(raw_sent)
    inverse = None
    for it in range(ITERS):
        first = it == 0

        def pair_copy(kz):
            return remote(
                s.pair_out.at[it, kz], s.pair_in.at[it, kz], s.pair_send.at[it, kz], s.pair_recv.at[it, kz], to(1, 0)
            )

        def line_copy(kz):
            return remote(
                s.line_out.at[it, kz], s.line_in.at[it, kz], s.line_send.at[it, kz], s.line_recv.at[it, kz], to(2 * kz, 0)
            )

        if not first:

            @pl.loop(0, nd)
            def _(kd):
                s.panel[kd] = panel_of(it, kd, (0,), None)

            band_sent[1].wait_recv()

            @pl.loop(0, nd)
            def _(kd):
                s.panel[kd] = panel_of(it, kd, (1,), s.panel[kd])

            gram_sent_two = gram_middle(it - 1, gram_sent)
            gather_relay(s.band.at[it], s.band_send, s.band_recv, band_sent)

            @pl.loop(0, nd)
            def _(kd):
                s.panel[kd] = panel_of(it, kd, (2,), s.panel[kd])

            band_sent[2].wait_recv()

        sources = tuple(range(nb)) if first else (nb - 1,)


        @pl.loop(0, nz)
        def _(at):
            kz = nz - 1 - at
            kd = 2 * kz + 1
            total = panel_of(it, kd, sources, None if first else s.panel[kd])
            s.pair_out[it, kz] = total.astype(BF16)
            pair_copy(kz).start()

        @pl.loop(0, nz - 1)
        def _(at):
            kz = nz - 1 - at
            kd = 2 * kz
            total = panel_of(it, kd, sources, None if first else s.panel[kd])
            pair_copy(kz).wait_recv()
            s.line_out[it, kz] = (total + s.pair_in[it, kz].astype(F32)).astype(BF16)
            line_copy(kz).start()

        whole = panel_of(it, 0, sources, None if first else s.panel[0])
        if not first:
            gram = gram_end(it - 1, gram_sent_two)
            inverse = inverse_factor(gram, k_vec)
            waits += gram_sent_two
        pair_copy(0).wait_recv()
        whole = whole + s.pair_in[it, 0].astype(F32)
        for kz in range(1, nz):
            line_copy(kz).wait_recv()
            whole = whole + s.line_in[it, kz].astype(F32)
        if first:
            for copy in size_sent:
                copy.wait()
            size = s.size[me_d]
            for k in range(1, nd):
                size = size + s.size_from[k]
            weight_own = jnp.concatenate([s.weight[pl.ds(me_d * col_per + h, 1), :] for h in range(col_per)], axis=1)
            scale = weight_own / jnp.maximum(size, 1.0)
        else:
            whole = jnp.dot(inverse, whole, precision=highest, preferred_element_type=F32)
        s.weighted[it, 0, 0] = (whole * scale).astype(BF16)

        def line_gather(kz):
            return remote(
                s.weighted.at[it, 0, 0], s.weighted.at[it, kz, 0], s.wt_send.at[it, kz, 0], s.wt_recv.at[it, kz, 0], to(2 * kz, 0)
            )

        def pair_gather(kz):
            return remote(
                s.weighted.at[it, kz, 0], s.weighted.at[it, kz, 1], s.wt_send.at[it, kz, 1], s.wt_recv.at[it, kz, 1], to(1, 0)
            )

        for kz in range(nz - 1, 0, -1):
            line_gather(kz).start()
        pair_gather(0).start()

        def source(kz, side):
            return flip(me_d, 2 * kz + side, d_bits)

        for q in range(nb):
            s.image[q] = image_of(q, s.weighted[it, 0, 0], me_d)

        @pl.loop(1, nz)
        def _(kz):
            line_gather(kz).wait_recv()
            pair_gather(kz).start()
            pair_gather(kz - 1).wait_recv()
            for q in range(nb):
                s.image[q] += image_of(q, s.weighted[it, kz - 1, 1], source(kz - 1, 1)) + image_of(
                    q, s.weighted[it, kz, 0], source(kz, 0)
                )

        pair_gather(nz - 1).wait_recv()

        def finish(k):
            q = flip(me_b, k, b_bits)
            return s.image[q] + image_of(q, s.weighted[it, nz - 1, 1], source(nz - 1, 1))

        def mate_copy(k):
            return remote(
                s.mate_out.at[it, k], s.mate_in.at[it, k], s.mate_send.at[it, k], s.mate_recv.at[it, k], to(0, 1)
            )

        far_copy = remote(s.far_out.at[it], s.far_in.at[it], s.far_send.at[it], s.far_recv.at[it], to(0, 2))
        s.mate_out[it, 1] = finish(3).astype(BF16)
        mate_copy(1).start()
        both = finish(2)
        mate_copy(1).wait_recv()
        s.far_out[it] = (both + s.mate_in[it, 1].astype(F32)).astype(BF16)
        far_copy.start()
        s.mate_out[it, 0] = finish(1).astype(BF16)
        mate_copy(0).start()
        image = finish(0)
        mate_copy(0).wait_recv()
        image = image + s.mate_in[it, 0].astype(F32)
        far_copy.wait_recv()
        image = image + s.far_in[it].astype(F32)
        image = jnp.concatenate(
            [image[:, i * tile : (i + 1) * tile] * inv_own[i : i + 1] for i in range(row_per)], axis=1
        )
        more = it + 1 < ITERS
        if more:
            s.band[it + 1, 0] = jnp.concatenate(
                [image[:, i * tile : (i + 1) * tile] * inv_own[i : i + 1] for i in range(row_per)], axis=1
            ).astype(BF16)
            band_sent = gather_start(s.band.at[it + 1], s.band_send, s.band_recv)
            waits += band_sent[:]
        gram_sent = gram_start(it, image)
        waits += gram_sent
        if not more:
            gram_sent_two = gram_middle(it, gram_sent)
            waits += gram_sent_two
            gram = gram_end(it, gram_sent_two)
            inverse = inverse_factor(gram, k_vec)
            out_ref[...] = jnp.dot(inverse, image, precision=highest, preferred_element_type=F32)
        for k in range(2):
            mate_copy(k).wait_send()
        far_copy.wait_send()
        for kz in range(nz):
            pair_copy(kz).wait_send()
            pair_gather(kz).wait_send()
        for kz in range(1, nz):
            line_copy(kz).wait_send()
            line_gather(kz).wait_send()
    for copy in waits:
        copy.wait_send()
    remote(s.band.at[1, 2], s.band.at[1, 3], s.band_send.at[3], s.band_recv.at[3], to(0, 1)).wait_send()


def scratch_of(nd, nb, slots, tile, k_vec, own_rows, own_cols):
    dma = pltpu.SemaphoreType.DMA
    row_tiles, col_tiles = own_rows * nb // tile, own_cols * nd // tile
    nz = nd // 2
    fold = (k_vec // 2, 2 * k_vec)
    buffers = {
        "tiles": ((slots, tile, tile), I32),
        "bits": ((slots + 1, tile, tile), BF16),
        "size_terms": ((slots + 1, 8, tile), F32),
        "doc_terms": ((slots + 1, 8, tile), F32),
        "table": ((8, tile), I32),
        "start": ((k_vec, own_rows), F32),
        "weight": ((col_tiles, tile), F32),
        "weight_terms": ((2, col_tiles, 16, tile), BF16),
        "degree_own": ((row_tiles, tile), F32),
        "degree": ((nb, row_tiles, tile), F32),
        "inv": ((row_tiles, tile), F32),
        "size": ((nd, 1, own_cols), F32),
        "size_from": ((nd, 1, own_cols), F32),
        "raw": ((nb, k_vec, own_rows), BF16),
        "band": ((ITERS, nb, k_vec, own_rows), BF16),
        "panel": ((nd, k_vec, own_cols), F32),
        "pair_out": ((ITERS, nz, k_vec, own_cols), BF16),
        "pair_in": ((ITERS, nz, k_vec, own_cols), BF16),
        "line_out": ((ITERS, nz, k_vec, own_cols), BF16),
        "line_in": ((ITERS, nz, k_vec, own_cols), BF16),
        "weighted": ((ITERS, nz, 2, k_vec, own_cols), BF16),
        "image": ((nb, k_vec, own_rows), F32),
        "mate_out": ((ITERS, 2, k_vec, own_rows), BF16),
        "mate_in": ((ITERS, 2, k_vec, own_rows), BF16),
        "far_out": ((ITERS, k_vec, own_rows), BF16),
        "far_in": ((ITERS, k_vec, own_rows), BF16),
        "gram_one": ((ITERS, 2 * nb) + fold, F32),
        "gram_two": ((ITERS, nz) + fold, F32),
    }
    total = 0
    for shape, kind in buffers.values():
        count = jnp.dtype(kind).itemsize
        for extent in shape:
            count *= extent
        total += count
    scratch = {name: pltpu.VMEM(shape, kind) for name, (shape, kind) in buffers.items()}
    scratch["slot"] = pltpu.SMEM((8, tile), I32)
    sems = {"small_sem": (3,), "load_sem": (CHUNKS,)}
    for name, shape in {
        "raw": (nb,),
        "deg": (nb,),
        "size": (nd,),
        "band": (nb,),
        "pair": (ITERS, nz),
        "line": (ITERS, nz),
        "wt": (ITERS, nz, 2),
        "mate": (ITERS, 2),
        "far": (ITERS,),
        "g1": (ITERS, 2 * nb),
        "g2": (ITERS, nz),
    }.items():
        sems[name + "_send"] = shape
        sems[name + "_recv"] = shape
    for name, shape in sems.items():
        scratch[name] = dma(shape)
    return scratch, total


VMEM_BYTES = 60000 * 1024


def body(start_vectors, bucket_weight, tile_count, tile_coords, patterns):
    nd, nb = lax.axis_size("doc"), lax.axis_size("bkt")
    slots, tile = patterns.shape[2], patterns.shape[3]
    k_vec, own_rows = start_vectors.shape
    band_cols = bucket_weight.shape[0]
    own_cols = band_cols // nd
    scratch, total = scratch_of(nd, nb, slots, tile, k_vec, own_rows, own_cols)
    fits = total + 4 * k_vec * own_rows * 4 < VMEM_BYTES
    powers = nd & (nd - 1) == 0 and nd >= 4 and nb == 4
    whole = band_cols == nd * own_cols and own_cols == 2 * tile and 2 * k_vec == tile
    table = own_rows % (2 * tile) == 0 and own_rows // tile * (band_cols // tile) == tile and own_rows // tile % 8 == 0
    if not (fits and powers and whole and table and slots % (CHUNKS * GROUP) == 0):
        return plain_body(start_vectors, bucket_weight, tile_count, tile_coords, patterns)
    smem = pl.BlockSpec(memory_space=pltpu.SMEM)
    vmem = pl.BlockSpec(memory_space=pltpu.VMEM)
    anywhere = pl.BlockSpec(memory_space=pl.ANY)
    coords = tile_coords.reshape(slots, 2).T
    return pl.pallas_call(
        functools.partial(kernel, tuple(scratch), nd, nb),
        out_shape=jax.ShapeDtypeStruct((k_vec, own_rows), F32),
        in_specs=[smem, smem, vmem, anywhere, anywhere, anywhere],
        out_specs=vmem,
        scratch_shapes=list(scratch.values()),
        compiler_params=pltpu.CompilerParams(
            collective_id=0, has_side_effects=True, vmem_limit_bytes=VMEM_BYTES
        ),
        name="subspace",
    )(tile_count, coords, coords, start_vectors, bucket_weight.reshape(band_cols // tile, tile), patterns.reshape(slots, tile, tile))


def solution(mesh):
    in_specs = (
        P(None, ("doc", "bkt")),
        P("bkt"),
        P("doc", "bkt"),
        P("doc", "bkt", None, None),
        P("doc", "bkt", None, None, None),
    )
    out_specs = P(None, ("doc", "bkt"))
    return jax.shard_map(body, mesh=mesh, in_specs=in_specs, out_specs=out_specs, check_vma=False)
```

```python
import functools
import types

import jax
import jax.numpy as jnp
from jax import lax
from jax.experimental import pallas as pl
from jax.experimental.pallas import tpu as pltpu
from jax.sharding import PartitionSpec as P

ITERS = 2


def plain_body(start_vectors, bucket_weight, tile_count, tile_coords, patterns):
    highest = lax.Precision.HIGHEST
    slot_total = patterns.shape[2]
    tile_size = patterns.shape[3]
    vector_count = start_vectors.shape[0]
    own_rows = start_vectors.shape[1]
    band_rows = own_rows * lax.axis_size("bkt")
    band_cols = bucket_weight.shape[0]
    row_tiles = band_rows // tile_size
    col_tiles = band_cols // tile_size
    total_docs = band_rows * lax.axis_size("doc")
    live_slot = (jnp.arange(slot_total) < tile_count[0, 0]).astype(jnp.int32)
    pattern_int = patterns[0, 0] * live_slot[:, None, None]
    pattern = pattern_int.astype(jnp.bfloat16)
    row_index = tile_coords[0, 0, :, 0]
    col_index = tile_coords[0, 0, :, 1]
    row_pick = jnp.arange(row_tiles)[:, None] == row_index[None, :]
    col_pick = jnp.arange(col_tiles)[:, None] == col_index[None, :]
    row_pick_f = row_pick.astype(jnp.float32)
    row_pick_b = row_pick.astype(jnp.bfloat16)
    col_pick_f = col_pick.astype(jnp.float32)
    col_pick_b = col_pick.astype(jnp.bfloat16)
    pattern_f = pattern_int.astype(jnp.float32)
    weight_tiles = bucket_weight.reshape(col_tiles, tile_size)
    slot_weight = jnp.dot(col_pick_f.T, weight_tiles, precision=highest)
    row_part = jnp.einsum("tij,tj->ti", pattern_f, slot_weight, precision=highest)
    doc_part = jnp.dot(row_pick_f, row_part, precision=highest).reshape(band_rows)
    col_part = jnp.sum(pattern_f, axis=1)
    bucket_part = jnp.dot(col_pick_f, col_part, precision=highest).reshape(band_cols)
    doc_degree = lax.psum(doc_part, "bkt")
    bucket_size = lax.psum(bucket_part.astype(jnp.bfloat16), "doc").astype(jnp.float32)
    inv_band = 1.0 / jnp.sqrt(jnp.maximum(doc_degree, 1.0))
    inv_own = lax.dynamic_slice_in_dim(inv_band, lax.axis_index("bkt") * own_rows, own_rows)
    bucket_scale = bucket_weight / jnp.maximum(bucket_size, 1.0)
    vectors = start_vectors
    for sweep_index in range(ITERS):
        scaled = (vectors * inv_own[None, :]).astype(jnp.bfloat16)
        band_vecs = lax.all_gather(scaled, "bkt", axis=1, tiled=True)
        picked = jnp.einsum(
            "rt,kri->kti",
            row_pick_b,
            band_vecs.reshape(vector_count, row_tiles, tile_size),
            preferred_element_type=jnp.float32,
        ).astype(jnp.bfloat16)
        products = jnp.einsum("kti,tij->ktj", picked, pattern, preferred_element_type=jnp.float32)
        panel_part = (
            jnp.zeros((vector_count, col_tiles, tile_size), jnp.float32)
            .at[:, col_index, :]
            .add(products)
        )
        panel_part = panel_part.reshape(vector_count, band_cols)
        panel_whole = lax.psum(panel_part, "doc")
        weighted = (panel_whole * bucket_scale[None, :]).astype(jnp.bfloat16)
        spread = jnp.einsum(
            "ct,kcj->ktj",
            col_pick_b,
            weighted.reshape(vector_count, col_tiles, tile_size),
            preferred_element_type=jnp.float32,
        ).astype(jnp.bfloat16)
        returned = jnp.einsum("ktj,tij->kti", spread, pattern, preferred_element_type=jnp.float32)
        row_terms = (
            jnp.zeros((vector_count, row_tiles, tile_size), jnp.float32)
            .at[:, row_index, :]
            .add(returned)
        )
        row_terms = row_terms.reshape(vector_count, band_rows)
        rows_own = (
            lax.psum_scatter(row_terms, "bkt", scatter_dimension=1, tiled=True) * inv_own[None, :]
        )
        gram_local = jnp.dot(rows_own, rows_own.T, precision=highest)
        gram_matrix = lax.psum(gram_local, ("doc", "bkt")) / total_docs
        factor = jnp.linalg.cholesky(gram_matrix)
        vectors = lax.linalg.triangular_solve(factor, rows_own, left_side=True, lower=True)
    return vectors


MESH = pl.DeviceIdType.MESH
F32 = jnp.float32
BF16 = jnp.bfloat16
I32 = jnp.int32
NT = (((1,), (1,)), ((), ()))
BLOCK = 4
CHUNKS = 8
GROUP = 16


def flip(value, k, bits):
    out = 0
    for at in range(bits):
        unit = 1 << at
        bit = lax.rem(lax.div(value, unit), 2)
        want = (k >> at) & 1 if isinstance(k, int) else lax.rem(lax.div(k, unit), 2)
        out = out + unit * (bit + want - 2 * bit * want)
    return out


def inverse_factor(gram, k_vec):
    row_at = lax.broadcasted_iota(I32, (k_vec, k_vec), 0)
    col_at = lax.broadcasted_iota(I32, (k_vec, k_vec), 1)
    eye = (row_at == col_at).astype(F32)
    work = jnp.concatenate([gram, eye], axis=1)
    for at in range(0, k_vec, BLOCK):
        top = at // 8 * 8
        part = work[top:]
        below = lax.broadcasted_iota(I32, part.shape, 0)
        cols = [jnp.broadcast_to(part[:, at + m : at + m + 1], part.shape) for m in range(BLOCK)]
        for m in range(BLOCK):
            row = at - top + m
            factor = jnp.where(below > row, cols[m] * (1.0 / cols[m][row : row + 1]), 0.0)
            part = part - factor * part[row : row + 1]
            for n in range(m + 1, BLOCK):
                cols[n] = cols[n] - factor * cols[n][row : row + 1]
        work = jnp.concatenate([work[:top], part], axis=0) if top else part
    pivots = jnp.sum(work[:, :k_vec] * eye, axis=1, keepdims=True)
    return work[:, k_vec:] / jnp.sqrt(pivots)


def kernel(names, nd, nb, count_ref, coord_ref, place_ref, start_ref, weight_ref, patterns_hbm, out_ref, *refs):
    s = types.SimpleNamespace(**dict(zip(names, refs, strict=True)))
    highest = lax.Precision.HIGHEST
    me_d = lax.axis_index("doc")
    me_b = lax.axis_index("bkt")
    d_bits, b_bits = nd.bit_length() - 1, nb.bit_length() - 1
    slots, tile = patterns_hbm.shape[0], patterns_hbm.shape[1]
    k_vec, own_rows = start_ref.shape
    col_tiles = weight_ref.shape[0]
    col_per = col_tiles // nd
    row_per = own_rows // tile
    own_cols = col_per * tile
    total_docs = own_rows * nb * nd
    nz = nd // 2

    def to(kd, kb):
        return {"doc": flip(me_d, kd, d_bits), "bkt": flip(me_b, kb, b_bits)}

    def remote(src, dst, ssem, rsem, peer):
        return pltpu.make_async_remote_copy(
            src_ref=src, dst_ref=dst, send_sem=ssem, recv_sem=rsem,
            device_id=peer, device_id_type=MESH,
        )

    def send(*args):
        copy = remote(*args)
        copy.start()
        return copy

    per_chunk = slots // CHUNKS

    def load(c):
        part = pl.ds(c * per_chunk, per_chunk)
        return pltpu.make_async_copy(patterns_hbm.at[part], s.tiles.at[part], s.load_sem.at[c])

    for c in range(CHUNKS):
        load(c).start()

    barrier = pltpu.get_barrier_semaphore()
    peers = [(kd, kb) for kd in range(nd) for kb in range(nb) if (kd < 2 or kb == 0) and kd + kb]
    for kd, kb in peers:
        pl.semaphore_signal(barrier, inc=1, device_id=to(kd, kb), device_id_type=MESH)

    lane = lax.broadcasted_iota(I32, (1, slots), 1)
    place = place_ref[0:1, :] * col_tiles + place_ref[1:2, :]
    place = jnp.where(lane < count_ref[0, 0], place, -1)
    across = jnp.transpose(jnp.broadcast_to(place, (tile, slots)))
    position = lax.broadcasted_iota(I32, (slots, tile), 1)
    slot_at = lax.broadcasted_iota(I32, (slots, tile), 0)
    for b in range(nb):
        found = jnp.max(jnp.where(across == position + b * tile, slot_at, -1), axis=0, keepdims=True)
        s.table[b : b + 1, :] = jnp.where(found >= 0, found, slots)
    tables = pltpu.make_async_copy(s.table, s.slot, s.table_sem)
    tables.start()
    s.bits[slots] = jnp.zeros((tile, tile), BF16)
    s.turned[slots] = jnp.zeros((tile, tile), BF16)
    s.size_terms[slots] = jnp.zeros((8, tile), F32)
    s.doc_terms[slots] = jnp.zeros((8, tile), F32)

    for c in range(col_tiles):
        left = weight_ref[c : c + 1, :]
        terms = []
        for _ in range(3):
            terms.append(left.astype(BF16).astype(F32))
            left = left - terms[-1]
        zeros = jnp.zeros((5, tile), F32)
        gap = jnp.zeros((8, tile), F32)
        eight = jnp.concatenate(terms + [zeros], axis=0)
        s.weight_terms[0, c] = jnp.concatenate([eight, gap], axis=0).astype(BF16)
        s.weight_terms[1, c] = jnp.concatenate([gap, eight], axis=0).astype(BF16)
    s.raw[0] = start_ref[...].astype(BF16)
    pl.semaphore_wait(barrier, len(peers))

    def gather_start(buf, ssem, rsem):
        return [
            send(buf.at[0], buf.at[k], ssem.at[k], rsem.at[k], to(0, k))
            for k in (2, 1)
        ]

    def gather_relay(buf, ssem, rsem, sent):
        sent[0].wait_recv()
        sent.append(send(buf.at[2], buf.at[3], ssem.at[3], rsem.at[3], to(0, 1)))

    waits = gather_start(s.raw, s.raw_send, s.raw_recv)
    raw_sent = waits


    @pl.loop(0, CHUNKS)
    def _(c):
        load(c).wait()

        @pl.loop(0, per_chunk // GROUP)
        def _(g):
            base = c * per_chunk + g * GROUP
            for u in range(0, GROUP, 2):
                pair = []
                for v in range(2):
                    at = base + u + v
                    block = s.tiles[at].astype(F32)
                    s.size_terms[at] = jnp.sum(block.reshape(tile // 8, 8, tile), axis=0)
                    block = block.astype(BF16)
                    s.bits[at] = block
                    pair.append(jnp.transpose(block))
                    s.turned[at] = pair[v]
                left = jnp.concatenate(
                    [s.weight_terms[0, coord_ref[1, base + u]], s.weight_terms[1, coord_ref[1, base + u + 1]]], axis=1
                )
                sums = jnp.dot(left, jnp.concatenate(pair, axis=0), preferred_element_type=F32)
                s.doc_terms[base + u] = sums[:8]
                s.doc_terms[base + u + 1] = sums[8:]

    tables.wait()
    gather_relay(s.raw, s.raw_send, s.raw_recv, raw_sent)

    def slot_of(b, i, c):
        return s.slot[b, i * col_tiles + c]

    for b in range(nb):
        for i in range(row_per):
            total = s.doc_terms[slot_of(b, i, 0)]
            for c in range(1, col_tiles):
                total = total + s.doc_terms[slot_of(b, i, c)]
            s.degree_own[b * row_per + i : b * row_per + i + 1, :] = total[0:1] + total[1:2] + total[2:3]
    s.degree[me_b] = s.degree_own[...]
    degree_sent = [
        send(s.degree.at[me_b], s.degree.at[me_b], s.deg_send.at[k], s.deg_recv.at[k], to(0, k))
        for k in range(nb - 1, 0, -1)
    ]
    for c in range(col_tiles):
        total = s.size_terms[slot_of(0, 0, c)]
        for b in range(nb):
            for i in range(0 if b else 1, row_per):
                total = total + s.size_terms[slot_of(b, i, c)]
        total = jnp.sum(total, axis=0, keepdims=True)
        s.size[c // col_per, :, c % col_per * tile : (c % col_per + 1) * tile] = total
    size_sent = []
    for k in range(nd - 1, 0, -1):
        size_sent.append(
            send(s.size.at[flip(me_d, k, d_bits)], s.size_from.at[k], s.size_send.at[k], s.size_recv.at[k], to(k, 0))
        )
    for copy in degree_sent:
        copy.wait()
    degree = s.degree[0]
    for b in range(1, nb):
        degree = degree + s.degree[b]
    s.inv[...] = 1.0 / jnp.sqrt(jnp.maximum(degree, 1.0))
    for copy in raw_sent[1:]:
        copy.wait_recv()
    for k in range(nb):
        first = flip(me_b, k, b_bits) * row_per
        inv_rows = s.inv[pl.ds(pl.multiple_of(first, row_per), row_per), :]
        for i in range(row_per):
            lanes = slice(i * tile, (i + 1) * tile)
            s.band[0, k, :, lanes] = (s.raw[k, :, lanes].astype(F32) * inv_rows[i : i + 1]).astype(BF16)
    inv_own = s.inv[pl.ds(pl.multiple_of(me_b * row_per, row_per), row_per), :]

    def tiles_of(b, i, o):
        pick = [[s.bits[slot_of(b, i + u, o * col_per + h)] for h in range(col_per)] for u in range(2)]
        return jnp.concatenate([jnp.concatenate(row, axis=1) for row in pick], axis=0)

    def panel_of(it, kd, sources, acc):
        o = flip(me_d, kd, d_bits)
        for k in sources:
            b = flip(me_b, k, b_bits)
            for i in range(0, row_per, 2):
                left = s.band[it, k, :, i * tile : (i + 2) * tile]
                term = jnp.dot(left, tiles_of(b, i, o), preferred_element_type=F32)
                acc = term if acc is None else acc + term
        return acc

    def image_of(q, left, o):
        rows = []
        for h in range(col_per):
            row = [s.turned[slot_of(q, i, o * col_per + h)] for i in range(row_per)]
            rows.append(jnp.concatenate(row, axis=1))
        return jnp.dot(left, jnp.concatenate(rows, axis=0), preferred_element_type=F32)

    def gram_start(it, image):
        high = image.astype(BF16)
        low = (image - high.astype(F32)).astype(BF16)
        both = jnp.concatenate([high, low], axis=0)
        gram = lax.dot_general(both, both, NT, preferred_element_type=F32)
        gram = gram[:k_vec] + gram[k_vec:]
        gram = gram[:, :k_vec] + gram[:, k_vec:]
        half = k_vec // 2
        mine = lax.rem(me_d, 2) * nb + me_b
        s.gram_one[it, mine] = jnp.concatenate([gram[:half], gram[half:]], axis=1)
        return [
            send(s.gram_one.at[it, mine], s.gram_one.at[it, mine], s.g1_send.at[it, k], s.g1_recv.at[it, k], to(k // nb, k % nb))
            for k in range(2 * nb - 1, 0, -1)
        ]

    def gram_middle(it, sent):
        for copy in sent:
            copy.wait_recv()
        total = s.gram_one[it, 0]
        for k in range(1, 2 * nb):
            total = total + s.gram_one[it, k]
        mine = lax.div(me_d, 2)
        s.gram_two[it, mine] = total
        return [
            send(s.gram_two.at[it, mine], s.gram_two.at[it, mine], s.g2_send.at[it, k], s.g2_recv.at[it, k], to(2 * k, 0))
            for k in range(nz - 1, 0, -1)
        ]

    def gram_end(it, sent):
        for copy in sent:
            copy.wait_recv()
        total = s.gram_two[it, 0]
        for k in range(1, nz):
            total = total + s.gram_two[it, k]
        return jnp.concatenate([total[:, :k_vec], total[:, k_vec:]], axis=0) / total_docs

    waits = list(raw_sent)
    inverse = None
    for it in range(ITERS):
        first = it == 0

        def pair_copy(kz):
            return remote(
                s.pair_out.at[it, kz], s.pair_in.at[it, kz], s.pair_send.at[it, kz], s.pair_recv.at[it, kz], to(1, 0)
            )

        def line_copy(kz):
            return remote(
                s.line_out.at[it, kz], s.line_in.at[it, kz], s.line_send.at[it, kz], s.line_recv.at[it, kz], to(2 * kz, 0)
            )

        if not first:

            @pl.loop(0, nd)
            def _(kd):
                s.panel[kd] = panel_of(it, kd, (0,), None)

            band_sent[1].wait_recv()

            @pl.loop(0, nd)
            def _(kd):
                s.panel[kd] = panel_of(it, kd, (1,), s.panel[kd])

            gather_relay(s.band.at[it], s.band_send, s.band_recv, band_sent)

            @pl.loop(0, nd)
            def _(kd):
                s.panel[kd] = panel_of(it, kd, (2,), s.panel[kd])

            gram_sent_two = gram_middle(it - 1, gram_sent)
            band_sent[2].wait_recv()

        sources = tuple(range(nb)) if first else (nb - 1,)


        @pl.loop(0, nz)
        def _(at):
            kz = nz - 1 - at
            kd = 2 * kz + 1
            total = panel_of(it, kd, sources, None if first else s.panel[kd])
            s.pair_out[it, kz] = total.astype(BF16)
            pair_copy(kz).start()

        @pl.loop(0, nz - 1)
        def _(at):
            kz = nz - 1 - at
            kd = 2 * kz
            total = panel_of(it, kd, sources, None if first else s.panel[kd])
            pair_copy(kz).wait_recv()
            s.line_out[it, kz] = (total + s.pair_in[it, kz].astype(F32)).astype(BF16)
            line_copy(kz).start()

        whole = panel_of(it, 0, sources, None if first else s.panel[0])
        if not first:
            gram = gram_end(it - 1, gram_sent_two)
            inverse = inverse_factor(gram, k_vec)
            waits += gram_sent_two
        pair_copy(0).wait_recv()
        whole = whole + s.pair_in[it, 0].astype(F32)
        for kz in range(1, nz):
            line_copy(kz).wait_recv()
            whole = whole + s.line_in[it, kz].astype(F32)
        if first:
            for copy in size_sent:
                copy.wait()
            size = s.size[me_d]
            for k in range(1, nd):
                size = size + s.size_from[k]
            weight_own = jnp.concatenate([weight_ref[pl.ds(me_d * col_per + h, 1), :] for h in range(col_per)], axis=1)
            scale = weight_own / jnp.maximum(size, 1.0)
        else:
            whole = jnp.dot(inverse, whole, precision=highest, preferred_element_type=F32)
        s.weighted[it, 0, 0] = (whole * scale).astype(BF16)

        def line_gather(kz):
            return remote(
                s.weighted.at[it, 0, 0], s.weighted.at[it, kz, 0], s.wt_send.at[it, kz, 0], s.wt_recv.at[it, kz, 0], to(2 * kz, 0)
            )

        def pair_gather(kz):
            return remote(
                s.weighted.at[it, kz, 0], s.weighted.at[it, kz, 1], s.wt_send.at[it, kz, 1], s.wt_recv.at[it, kz, 1], to(1, 0)
            )

        for kz in range(nz - 1, 0, -1):
            line_gather(kz).start()
        pair_gather(0).start()

        def source(kz, side):
            return flip(me_d, 2 * kz + side, d_bits)

        for q in range(nb):
            s.image[q] = image_of(q, s.weighted[it, 0, 0], me_d)

        @pl.loop(1, nz)
        def _(kz):
            line_gather(kz).wait_recv()
            pair_gather(kz).start()
            pair_gather(kz - 1).wait_recv()
            for q in range(nb):
                s.image[q] += image_of(q, s.weighted[it, kz - 1, 1], source(kz - 1, 1)) + image_of(
                    q, s.weighted[it, kz, 0], source(kz, 0)
                )

        pair_gather(nz - 1).wait_recv()

        def finish(k):
            q = flip(me_b, k, b_bits)
            return s.image[q] + image_of(q, s.weighted[it, nz - 1, 1], source(nz - 1, 1))

        def mate_copy(k):
            return remote(
                s.mate_out.at[it, k], s.mate_in.at[it, k], s.mate_send.at[it, k], s.mate_recv.at[it, k], to(0, 1)
            )

        far_copy = remote(s.far_out.at[it], s.far_in.at[it], s.far_send.at[it], s.far_recv.at[it], to(0, 2))
        s.mate_out[it, 1] = finish(3).astype(BF16)
        mate_copy(1).start()
        both = finish(2)
        mate_copy(1).wait_recv()
        s.far_out[it] = (both + s.mate_in[it, 1].astype(F32)).astype(BF16)
        far_copy.start()
        s.mate_out[it, 0] = finish(1).astype(BF16)
        mate_copy(0).start()
        image = finish(0)
        mate_copy(0).wait_recv()
        image = image + s.mate_in[it, 0].astype(F32)
        far_copy.wait_recv()
        image = image + s.far_in[it].astype(F32)
        image = jnp.concatenate(
            [image[:, i * tile : (i + 1) * tile] * inv_own[i : i + 1] for i in range(row_per)], axis=1
        )
        more = it + 1 < ITERS
        if more:
            s.band[it + 1, 0] = jnp.concatenate(
                [image[:, i * tile : (i + 1) * tile] * inv_own[i : i + 1] for i in range(row_per)], axis=1
            ).astype(BF16)
            band_sent = gather_start(s.band.at[it + 1], s.band_send, s.band_recv)
            waits += band_sent[:]
        gram_sent = gram_start(it, image)
        waits += gram_sent
        if not more:
            gram_sent_two = gram_middle(it, gram_sent)
            waits += gram_sent_two
            gram = gram_end(it, gram_sent_two)
            inverse = inverse_factor(gram, k_vec)
            out_ref[...] = jnp.dot(inverse, image, precision=highest, preferred_element_type=F32)
        for k in range(2):
            mate_copy(k).wait_send()
        far_copy.wait_send()
        for kz in range(nz):
            pair_copy(kz).wait_send()
            pair_gather(kz).wait_send()
        for kz in range(1, nz):
            line_copy(kz).wait_send()
            line_gather(kz).wait_send()
    for copy in waits:
        copy.wait_send()
    remote(s.band.at[1, 2], s.band.at[1, 3], s.band_send.at[3], s.band_recv.at[3], to(0, 1)).wait_send()


def scratch_of(nd, nb, slots, tile, k_vec, own_rows, own_cols):
    dma = pltpu.SemaphoreType.DMA
    row_tiles, col_tiles = own_rows * nb // tile, own_cols * nd // tile
    nz = nd // 2
    fold = (k_vec // 2, 2 * k_vec)
    buffers = {
        "tiles": ((slots, tile, tile), I32),
        "bits": ((slots + 1, tile, tile), BF16),
        "turned": ((slots + 1, tile, tile), BF16),
        "size_terms": ((slots + 1, 8, tile), F32),
        "doc_terms": ((slots + 1, 8, tile), F32),
        "table": ((8, tile), I32),
        "weight_terms": ((2, col_tiles, 16, tile), BF16),
        "degree_own": ((row_tiles, tile), F32),
        "degree": ((nb, row_tiles, tile), F32),
        "inv": ((row_tiles, tile), F32),
        "size": ((nd, 1, own_cols), F32),
        "size_from": ((nd, 1, own_cols), F32),
        "raw": ((nb, k_vec, own_rows), BF16),
        "band": ((ITERS, nb, k_vec, own_rows), BF16),
        "panel": ((nd, k_vec, own_cols), F32),
        "pair_out": ((ITERS, nz, k_vec, own_cols), BF16),
        "pair_in": ((ITERS, nz, k_vec, own_cols), BF16),
        "line_out": ((ITERS, nz, k_vec, own_cols), BF16),
        "line_in": ((ITERS, nz, k_vec, own_cols), BF16),
        "weighted": ((ITERS, nz, 2, k_vec, own_cols), BF16),
        "image": ((nb, k_vec, own_rows), F32),
        "mate_out": ((ITERS, 2, k_vec, own_rows), BF16),
        "mate_in": ((ITERS, 2, k_vec, own_rows), BF16),
        "far_out": ((ITERS, k_vec, own_rows), BF16),
        "far_in": ((ITERS, k_vec, own_rows), BF16),
        "gram_one": ((ITERS, 2 * nb) + fold, F32),
        "gram_two": ((ITERS, nz) + fold, F32),
    }
    total = 0
    for shape, kind in buffers.values():
        count = jnp.dtype(kind).itemsize
        for extent in shape:
            count *= extent
        total += count
    scratch = {name: pltpu.VMEM(shape, kind) for name, (shape, kind) in buffers.items()}
    scratch["slot"] = pltpu.SMEM((8, tile), I32)
    sems = {"load_sem": (CHUNKS,)}
    for name, shape in {
        "raw": (nb,),
        "deg": (nb,),
        "size": (nd,),
        "band": (nb,),
        "pair": (ITERS, nz),
        "line": (ITERS, nz),
        "wt": (ITERS, nz, 2),
        "mate": (ITERS, 2),
        "far": (ITERS,),
        "g1": (ITERS, 2 * nb),
        "g2": (ITERS, nz),
    }.items():
        sems[name + "_send"] = shape
        sems[name + "_recv"] = shape
    for name, shape in sems.items():
        scratch[name] = dma(shape)
    scratch["table_sem"] = dma
    return scratch, total


VMEM_BYTES = 60000 * 1024


def body(start_vectors, bucket_weight, tile_count, tile_coords, patterns):
    nd, nb = lax.axis_size("doc"), lax.axis_size("bkt")
    slots, tile = patterns.shape[2], patterns.shape[3]
    k_vec, own_rows = start_vectors.shape
    band_cols = bucket_weight.shape[0]
    own_cols = band_cols // nd
    scratch, total = scratch_of(nd, nb, slots, tile, k_vec, own_rows, own_cols)
    fits = total + 4 * k_vec * own_rows * 4 < VMEM_BYTES
    powers = nd & (nd - 1) == 0 and nd >= 4 and nb == 4
    whole = band_cols == nd * own_cols and own_cols == 2 * tile and 2 * k_vec == tile
    table = own_rows % (2 * tile) == 0 and own_rows // tile * (band_cols // tile) == tile and own_rows // tile % 8 == 0
    if not (fits and powers and whole and table and slots % (CHUNKS * GROUP) == 0):
        return plain_body(start_vectors, bucket_weight, tile_count, tile_coords, patterns)
    smem = pl.BlockSpec(memory_space=pltpu.SMEM)
    vmem = pl.BlockSpec(memory_space=pltpu.VMEM)
    anywhere = pl.BlockSpec(memory_space=pl.ANY)
    coords = tile_coords.reshape(slots, 2).T
    return pl.pallas_call(
        functools.partial(kernel, tuple(scratch), nd, nb),
        out_shape=jax.ShapeDtypeStruct((k_vec, own_rows), F32),
        in_specs=[smem, smem, vmem, vmem, vmem, anywhere],
        out_specs=vmem,
        scratch_shapes=list(scratch.values()),
        compiler_params=pltpu.CompilerParams(
            collective_id=0, has_side_effects=True, vmem_limit_bytes=VMEM_BYTES
        ),
        name="subspace",
    )(tile_count, coords, coords, start_vectors, bucket_weight.reshape(band_cols // tile, tile), patterns.reshape(slots, tile, tile))


def solution(mesh):
    in_specs = (
        P(None, ("doc", "bkt")),
        P("bkt"),
        P("doc", "bkt"),
        P("doc", "bkt", None, None),
        P("doc", "bkt", None, None, None),
    )
    out_specs = P(None, ("doc", "bkt"))
    return jax.shard_map(body, mesh=mesh, in_specs=in_specs, out_specs=out_specs, check_vma=False)
```

```python
import functools
import types

import jax
import jax.numpy as jnp
from jax import lax
from jax.experimental import pallas as pl
from jax.experimental.pallas import tpu as pltpu
from jax.sharding import PartitionSpec as P

ITERS = 2


def plain_body(start_vectors, bucket_weight, tile_count, tile_coords, patterns):
    highest = lax.Precision.HIGHEST
    slot_total = patterns.shape[2]
    tile_size = patterns.shape[3]
    vector_count = start_vectors.shape[0]
    own_rows = start_vectors.shape[1]
    band_rows = own_rows * lax.axis_size("bkt")
    band_cols = bucket_weight.shape[0]
    row_tiles = band_rows // tile_size
    col_tiles = band_cols // tile_size
    total_docs = band_rows * lax.axis_size("doc")
    live_slot = (jnp.arange(slot_total) < tile_count[0, 0]).astype(jnp.int32)
    pattern_int = patterns[0, 0] * live_slot[:, None, None]
    pattern = pattern_int.astype(jnp.bfloat16)
    row_index = tile_coords[0, 0, :, 0]
    col_index = tile_coords[0, 0, :, 1]
    row_pick = jnp.arange(row_tiles)[:, None] == row_index[None, :]
    col_pick = jnp.arange(col_tiles)[:, None] == col_index[None, :]
    row_pick_f = row_pick.astype(jnp.float32)
    row_pick_b = row_pick.astype(jnp.bfloat16)
    col_pick_f = col_pick.astype(jnp.float32)
    col_pick_b = col_pick.astype(jnp.bfloat16)
    pattern_f = pattern_int.astype(jnp.float32)
    weight_tiles = bucket_weight.reshape(col_tiles, tile_size)
    slot_weight = jnp.dot(col_pick_f.T, weight_tiles, precision=highest)
    row_part = jnp.einsum("tij,tj->ti", pattern_f, slot_weight, precision=highest)
    doc_part = jnp.dot(row_pick_f, row_part, precision=highest).reshape(band_rows)
    col_part = jnp.sum(pattern_f, axis=1)
    bucket_part = jnp.dot(col_pick_f, col_part, precision=highest).reshape(band_cols)
    doc_degree = lax.psum(doc_part, "bkt")
    bucket_size = lax.psum(bucket_part.astype(jnp.bfloat16), "doc").astype(jnp.float32)
    inv_band = 1.0 / jnp.sqrt(jnp.maximum(doc_degree, 1.0))
    inv_own = lax.dynamic_slice_in_dim(inv_band, lax.axis_index("bkt") * own_rows, own_rows)
    bucket_scale = bucket_weight / jnp.maximum(bucket_size, 1.0)
    vectors = start_vectors
    for sweep_index in range(ITERS):
        scaled = (vectors * inv_own[None, :]).astype(jnp.bfloat16)
        band_vecs = lax.all_gather(scaled, "bkt", axis=1, tiled=True)
        picked = jnp.einsum(
            "rt,kri->kti",
            row_pick_b,
            band_vecs.reshape(vector_count, row_tiles, tile_size),
            preferred_element_type=jnp.float32,
        ).astype(jnp.bfloat16)
        products = jnp.einsum("kti,tij->ktj", picked, pattern, preferred_element_type=jnp.float32)
        panel_part = (
            jnp.zeros((vector_count, col_tiles, tile_size), jnp.float32)
            .at[:, col_index, :]
            .add(products)
        )
        panel_part = panel_part.reshape(vector_count, band_cols)
        panel_whole = lax.psum(panel_part, "doc")
        weighted = (panel_whole * bucket_scale[None, :]).astype(jnp.bfloat16)
        spread = jnp.einsum(
            "ct,kcj->ktj",
            col_pick_b,
            weighted.reshape(vector_count, col_tiles, tile_size),
            preferred_element_type=jnp.float32,
        ).astype(jnp.bfloat16)
        returned = jnp.einsum("ktj,tij->kti", spread, pattern, preferred_element_type=jnp.float32)
        row_terms = (
            jnp.zeros((vector_count, row_tiles, tile_size), jnp.float32)
            .at[:, row_index, :]
            .add(returned)
        )
        row_terms = row_terms.reshape(vector_count, band_rows)
        rows_own = (
            lax.psum_scatter(row_terms, "bkt", scatter_dimension=1, tiled=True) * inv_own[None, :]
        )
        gram_local = jnp.dot(rows_own, rows_own.T, precision=highest)
        gram_matrix = lax.psum(gram_local, ("doc", "bkt")) / total_docs
        factor = jnp.linalg.cholesky(gram_matrix)
        vectors = lax.linalg.triangular_solve(factor, rows_own, left_side=True, lower=True)
    return vectors


MESH = pl.DeviceIdType.MESH
F32 = jnp.float32
BF16 = jnp.bfloat16
I32 = jnp.int32
NT = (((1,), (1,)), ((), ()))
BLOCK = 4
CHUNKS = 8
GROUP = 16


def flip(value, k, bits):
    out = 0
    for at in range(bits):
        unit = 1 << at
        bit = lax.rem(lax.div(value, unit), 2)
        want = (k >> at) & 1 if isinstance(k, int) else lax.rem(lax.div(k, unit), 2)
        out = out + unit * (bit + want - 2 * bit * want)
    return out


def inverse_factor(gram, k_vec):
    row_at = lax.broadcasted_iota(I32, (k_vec, k_vec), 0)
    col_at = lax.broadcasted_iota(I32, (k_vec, k_vec), 1)
    eye = (row_at == col_at).astype(F32)
    work = jnp.concatenate([gram, eye], axis=1)
    for at in range(0, k_vec, BLOCK):
        top = at // 8 * 8
        part = work[top:]
        below = lax.broadcasted_iota(I32, part.shape, 0)
        cols = [jnp.broadcast_to(part[:, at + m : at + m + 1], part.shape) for m in range(BLOCK)]
        for m in range(BLOCK):
            row = at - top + m
            factor = jnp.where(below > row, cols[m] * (1.0 / cols[m][row : row + 1]), 0.0)
            part = part - factor * part[row : row + 1]
            for n in range(m + 1, BLOCK):
                cols[n] = cols[n] - factor * cols[n][row : row + 1]
        work = jnp.concatenate([work[:top], part], axis=0) if top else part
    pivots = jnp.sum(work[:, :k_vec] * eye, axis=1, keepdims=True)
    return work[:, k_vec:] / jnp.sqrt(pivots)


def kernel(names, nd, nb, count_ref, coord_ref, place_ref, start_ref, weight_ref, patterns_hbm, out_ref, *refs):
    s = types.SimpleNamespace(**dict(zip(names, refs, strict=True)))
    highest = lax.Precision.HIGHEST
    me_d = lax.axis_index("doc")
    me_b = lax.axis_index("bkt")
    d_bits, b_bits = nd.bit_length() - 1, nb.bit_length() - 1
    slots, tile = patterns_hbm.shape[0], patterns_hbm.shape[1]
    k_vec, own_rows = start_ref.shape
    col_tiles = weight_ref.shape[0]
    col_per = col_tiles // nd
    row_per = own_rows // tile
    own_cols = col_per * tile
    total_docs = own_rows * nb * nd
    nz = nd // 2

    def to(kd, kb):
        return {"doc": flip(me_d, kd, d_bits), "bkt": flip(me_b, kb, b_bits)}

    def remote(src, dst, ssem, rsem, peer):
        return pltpu.make_async_remote_copy(
            src_ref=src, dst_ref=dst, send_sem=ssem, recv_sem=rsem,
            device_id=peer, device_id_type=MESH,
        )

    def send(*args):
        copy = remote(*args)
        copy.start()
        return copy

    per_chunk = slots // CHUNKS

    def load(c):
        part = pl.ds(c * per_chunk, per_chunk)
        return pltpu.make_async_copy(patterns_hbm.at[part], s.tiles.at[part], s.load_sem.at[c])

    for c in range(CHUNKS):
        load(c).start()

    barrier = pltpu.get_barrier_semaphore()
    peers = [(kd, kb) for kd in range(nd) for kb in range(nb) if (kd < 2 or kb == 0) and kd + kb]
    for kd, kb in peers:
        pl.semaphore_signal(barrier, inc=1, device_id=to(kd, kb), device_id_type=MESH)

    lane = lax.broadcasted_iota(I32, (1, slots), 1)
    place = place_ref[0:1, :] * col_tiles + place_ref[1:2, :]
    place = jnp.where(lane < count_ref[0, 0], place, -1)
    across = jnp.transpose(jnp.broadcast_to(place, (tile, slots)))
    position = lax.broadcasted_iota(I32, (slots, tile), 1)
    slot_at = lax.broadcasted_iota(I32, (slots, tile), 0)
    for b in range(nb):
        found = jnp.max(jnp.where(across == position + b * tile, slot_at, -1), axis=0, keepdims=True)
        s.table[b : b + 1, :] = jnp.where(found >= 0, found, slots)
    tables = pltpu.make_async_copy(s.table, s.slot, s.table_sem)
    tables.start()
    s.bits[slots] = jnp.zeros((tile, tile), BF16)
    s.turned[slots] = jnp.zeros((tile, tile), BF16)
    s.size_terms[slots] = jnp.zeros((8, tile), F32)
    s.doc_terms[slots] = jnp.zeros((8, tile), F32)

    for c in range(col_tiles):
        left = weight_ref[c : c + 1, :]
        terms = []
        for _ in range(3):
            terms.append(left.astype(BF16).astype(F32))
            left = left - terms[-1]
        zeros = jnp.zeros((5, tile), F32)
        gap = jnp.zeros((8, tile), F32)
        eight = jnp.concatenate(terms + [zeros], axis=0)
        s.weight_terms[0, c] = jnp.concatenate([eight, gap], axis=0).astype(BF16)
        s.weight_terms[1, c] = jnp.concatenate([gap, eight], axis=0).astype(BF16)
    s.raw[0] = start_ref[...].astype(BF16)
    pl.semaphore_wait(barrier, len(peers))

    def gather_start(buf, ssem, rsem):
        return [
            send(buf.at[0], buf.at[k], ssem.at[k], rsem.at[k], to(0, k))
            for k in (2, 1)
        ]

    def gather_relay(buf, ssem, rsem, sent):
        sent[0].wait_recv()
        sent.append(send(buf.at[2], buf.at[3], ssem.at[3], rsem.at[3], to(0, 1)))

    waits = gather_start(s.raw, s.raw_send, s.raw_recv)
    raw_sent = waits


    def convert(c):
        load(c).wait()

        @pl.loop(0, per_chunk // GROUP)
        def _(g):
            base = c * per_chunk + g * GROUP
            for u in range(0, GROUP, 2):
                pair = []
                for v in range(2):
                    at = base + u + v
                    block = s.tiles[at].astype(F32)
                    s.size_terms[at] = jnp.sum(block.reshape(tile // 8, 8, tile), axis=0)
                    block = block.astype(BF16)
                    s.bits[at] = block
                    pair.append(jnp.transpose(block))
                    s.turned[at] = pair[v]
                left = jnp.concatenate(
                    [s.weight_terms[0, coord_ref[1, base + u]], s.weight_terms[1, coord_ref[1, base + u + 1]]], axis=1
                )
                sums = jnp.dot(left, jnp.concatenate(pair, axis=0), preferred_element_type=F32)
                s.doc_terms[base + u] = sums[:8]
                s.doc_terms[base + u + 1] = sums[8:]

    pl.loop(0, CHUNKS - 1)(convert)
    gather_relay(s.raw, s.raw_send, s.raw_recv, raw_sent)
    convert(CHUNKS - 1)
    tables.wait()

    def slot_of(b, i, c):
        return s.slot[b, i * col_tiles + c]

    for b in range(nb):
        for i in range(row_per):
            total = s.doc_terms[slot_of(b, i, 0)]
            for c in range(1, col_tiles):
                total = total + s.doc_terms[slot_of(b, i, c)]
            s.degree_own[b * row_per + i : b * row_per + i + 1, :] = total[0:1] + total[1:2] + total[2:3]
    s.degree[me_b] = s.degree_own[...]
    degree_sent = [
        send(s.degree.at[me_b], s.degree.at[me_b], s.deg_send.at[k], s.deg_recv.at[k], to(0, k))
        for k in range(nb - 1, 0, -1)
    ]
    for c in range(col_tiles):
        total = s.size_terms[slot_of(0, 0, c)]
        for b in range(nb):
            for i in range(0 if b else 1, row_per):
                total = total + s.size_terms[slot_of(b, i, c)]
        total = jnp.sum(total, axis=0, keepdims=True)
        s.size[c // col_per, :, c % col_per * tile : (c % col_per + 1) * tile] = total
    size_sent = []
    for k in range(nd - 1, 0, -1):
        size_sent.append(
            send(s.size.at[flip(me_d, k, d_bits)], s.size_from.at[k], s.size_send.at[k], s.size_recv.at[k], to(k, 0))
        )
    for copy in degree_sent:
        copy.wait()
    degree = s.degree[0]
    for b in range(1, nb):
        degree = degree + s.degree[b]
    s.inv[...] = 1.0 / jnp.sqrt(jnp.maximum(degree, 1.0))
    for copy in raw_sent[1:]:
        copy.wait_recv()
    for k in range(nb):
        first = flip(me_b, k, b_bits) * row_per
        inv_rows = s.inv[pl.ds(pl.multiple_of(first, row_per), row_per), :]
        for i in range(row_per):
            lanes = slice(i * tile, (i + 1) * tile)
            s.band[0, k, :, lanes] = (s.raw[k, :, lanes].astype(F32) * inv_rows[i : i + 1]).astype(BF16)
    inv_own = s.inv[pl.ds(pl.multiple_of(me_b * row_per, row_per), row_per), :]

    def tiles_of(b, i, o):
        pick = [[s.bits[slot_of(b, i + u, o * col_per + h)] for h in range(col_per)] for u in range(2)]
        return jnp.concatenate([jnp.concatenate(row, axis=1) for row in pick], axis=0)

    def panel_of(it, kd, sources, acc):
        o = flip(me_d, kd, d_bits)
        for k in sources:
            b = flip(me_b, k, b_bits)
            for i in range(0, row_per, 2):
                left = s.band[it, k, :, i * tile : (i + 2) * tile]
                term = jnp.dot(left, tiles_of(b, i, o), preferred_element_type=F32)
                acc = term if acc is None else acc + term
        return acc

    def image_of(q, left, o):
        rows = []
        for h in range(col_per):
            row = [s.turned[slot_of(q, i, o * col_per + h)] for i in range(row_per)]
            rows.append(jnp.concatenate(row, axis=1))
        return jnp.dot(left, jnp.concatenate(rows, axis=0), preferred_element_type=F32)

    def gram_of(image):
        high = image.astype(BF16)
        low = (image - high.astype(F32)).astype(BF16)
        both = jnp.concatenate([high, low], axis=0)
        gram = lax.dot_general(both, both, NT, preferred_element_type=F32)
        gram = gram[:k_vec] + gram[k_vec:]
        gram = gram[:, :k_vec] + gram[:, k_vec:]
        half = k_vec // 2
        return jnp.concatenate([gram[:half], gram[half:]], axis=1)

    steps = (to(0, 1), to(0, 2), to(1, 0))

    def gram_step(at, total):
        s.gram_out[at] = total
        return send(s.gram_out.at[at], s.gram_in.at[at], s.gs_send.at[at], s.gs_recv.at[at], steps[at])

    def gram_sum(at, copy):
        copy.wait_recv()
        return s.gram_out[at] + s.gram_in[at]

    def gram_start(it, image):
        mine = lax.rem(me_d, 2) * nb + me_b
        s.gram_one[it, mine] = gram_of(image)
        return [
            send(s.gram_one.at[it, mine], s.gram_one.at[it, mine], s.g1_send.at[it, k], s.g1_recv.at[it, k], to(k // nb, k % nb))
            for k in range(2 * nb - 1, 0, -1)
        ]

    def gram_middle(it, sent):
        for copy in sent:
            copy.wait_recv()
        total = s.gram_one[it, 0]
        for k in range(1, 2 * nb):
            total = total + s.gram_one[it, k]
        return gram_line(it, total)

    def gram_line(it, total):
        mine = lax.div(me_d, 2)
        s.gram_two[it, mine] = total
        return [
            send(s.gram_two.at[it, mine], s.gram_two.at[it, mine], s.g2_send.at[it, k], s.g2_recv.at[it, k], to(2 * k, 0))
            for k in range(nz - 1, 0, -1)
        ]

    def gram_end(it, sent):
        for copy in sent:
            copy.wait_recv()
        total = s.gram_two[it, 0]
        for k in range(1, nz):
            total = total + s.gram_two[it, k]
        return jnp.concatenate([total[:, :k_vec], total[:, k_vec:]], axis=0) / total_docs

    waits = list(raw_sent)
    inverse = None
    for it in range(ITERS):
        first = it == 0

        def pair_copy(kz):
            return remote(
                s.pair_out.at[it, kz], s.pair_in.at[it, kz], s.pair_send.at[it, kz], s.pair_recv.at[it, kz], to(1, 0)
            )

        def line_copy(kz):
            return remote(
                s.line_out.at[it, kz], s.line_in.at[it, kz], s.line_send.at[it, kz], s.line_recv.at[it, kz], to(2 * kz, 0)
            )

        if not first:

            @pl.loop(0, nd)
            def _(kd):
                s.panel[kd] = panel_of(it, kd, (0,), None)

            gram_copies = [gram_sent, gram_step(1, gram_sum(0, gram_sent))]
            band_sent[1].wait_recv()

            @pl.loop(0, nd)
            def _(kd):
                s.panel[kd] = panel_of(it, kd, (1,), s.panel[kd])

            gram_copies.append(gram_step(2, gram_sum(1, gram_copies[1])))
            gather_relay(s.band.at[it], s.band_send, s.band_recv, band_sent)

            @pl.loop(0, nd)
            def _(kd):
                s.panel[kd] = panel_of(it, kd, (2,), s.panel[kd])

            gram_sent_two = gram_line(it - 1, gram_sum(2, gram_copies[2]))
            waits += gram_copies
            band_sent[2].wait_recv()

        sources = tuple(range(nb)) if first else (nb - 1,)


        @pl.loop(0, nz)
        def _(at):
            kz = nz - 1 - at
            kd = 2 * kz + 1
            total = panel_of(it, kd, sources, None if first else s.panel[kd])
            s.pair_out[it, kz] = total.astype(BF16)
            pair_copy(kz).start()

        @pl.loop(0, nz - 1)
        def _(at):
            kz = nz - 1 - at
            kd = 2 * kz
            total = panel_of(it, kd, sources, None if first else s.panel[kd])
            pair_copy(kz).wait_recv()
            s.line_out[it, kz] = (total + s.pair_in[it, kz].astype(F32)).astype(BF16)
            line_copy(kz).start()

        whole = panel_of(it, 0, sources, None if first else s.panel[0])
        if not first:
            gram = gram_end(it - 1, gram_sent_two)
            inverse = inverse_factor(gram, k_vec)
            waits += gram_sent_two
        pair_copy(0).wait_recv()
        whole = whole + s.pair_in[it, 0].astype(F32)
        for kz in range(1, nz):
            line_copy(kz).wait_recv()
            whole = whole + s.line_in[it, kz].astype(F32)
        if first:
            for copy in size_sent:
                copy.wait()
            size = s.size[me_d]
            for k in range(1, nd):
                size = size + s.size_from[k]
            weight_own = jnp.concatenate([weight_ref[pl.ds(me_d * col_per + h, 1), :] for h in range(col_per)], axis=1)
            scale = weight_own / jnp.maximum(size, 1.0)
        else:
            whole = jnp.dot(inverse, whole, precision=highest, preferred_element_type=F32)
        s.weighted[it, 0, 0] = (whole * scale).astype(BF16)

        def line_gather(kz):
            return remote(
                s.weighted.at[it, 0, 0], s.weighted.at[it, kz, 0], s.wt_send.at[it, kz, 0], s.wt_recv.at[it, kz, 0], to(2 * kz, 0)
            )

        def pair_gather(kz):
            return remote(
                s.weighted.at[it, kz, 0], s.weighted.at[it, kz, 1], s.wt_send.at[it, kz, 1], s.wt_recv.at[it, kz, 1], to(1, 0)
            )

        for kz in range(nz - 1, 0, -1):
            line_gather(kz).start()
        pair_gather(0).start()

        def source(kz, side):
            return flip(me_d, 2 * kz + side, d_bits)

        def line_relay():
            return remote(
                s.weighted.at[it, 0, 1], s.weighted.at[it, 1, 1], s.wt_send.at[it, 1, 1], s.wt_recv.at[it, 1, 1], to(2, 0)
            )

        def add_block(kz, side, fresh=False):
            for q in range(nb):
                term = image_of(q, s.weighted[it, kz, side], source(kz, side))
                s.image[q] = term if fresh else s.image[q] + term

        add_block(0, 0, True)
        pair_gather(0).wait_recv()
        line_relay().start()
        add_block(0, 1)
        line_gather(1).wait_recv()
        add_block(1, 0)

        @pl.loop(2, nz)
        def _(kz):
            line_gather(kz).wait_recv()
            pair_gather(kz).start()
            add_block(kz, 0)

        line_relay().wait_recv()
        add_block(1, 1)

        @pl.loop(2, nz - 1)
        def _(kz):
            pair_gather(kz).wait_recv()
            add_block(kz, 1)

        pair_gather(nz - 1).wait_recv()

        def finish(k):
            q = flip(me_b, k, b_bits)
            return s.image[q] + image_of(q, s.weighted[it, nz - 1, 1], source(nz - 1, 1))

        def mate_copy(k):
            return remote(
                s.mate_out.at[it, k], s.mate_in.at[it, k], s.mate_send.at[it, k], s.mate_recv.at[it, k], to(0, 1)
            )

        far_copy = remote(s.far_out.at[it], s.far_in.at[it], s.far_send.at[it], s.far_recv.at[it], to(0, 2))
        s.mate_out[it, 1] = finish(3).astype(BF16)
        mate_copy(1).start()
        both = finish(2)
        mate_copy(1).wait_recv()
        s.far_out[it] = (both + s.mate_in[it, 1].astype(F32)).astype(BF16)
        far_copy.start()
        s.mate_out[it, 0] = finish(1).astype(BF16)
        mate_copy(0).start()
        image = finish(0)
        mate_copy(0).wait_recv()
        image = image + s.mate_in[it, 0].astype(F32)
        far_copy.wait_recv()
        image = image + s.far_in[it].astype(F32)
        image = jnp.concatenate(
            [image[:, i * tile : (i + 1) * tile] * inv_own[i : i + 1] for i in range(row_per)], axis=1
        )
        more = it + 1 < ITERS
        if more:
            s.band[it + 1, 0] = jnp.concatenate(
                [image[:, i * tile : (i + 1) * tile] * inv_own[i : i + 1] for i in range(row_per)], axis=1
            ).astype(BF16)
            band_sent = gather_start(s.band.at[it + 1], s.band_send, s.band_recv)
            waits += band_sent[:]
            gram_sent = gram_step(0, gram_of(image))
        else:
            gram_sent = gram_start(it, image)
            waits += gram_sent
            gram_sent_two = gram_middle(it, gram_sent)
            waits += gram_sent_two
            gram = gram_end(it, gram_sent_two)
            inverse = inverse_factor(gram, k_vec)
            out_ref[...] = jnp.dot(inverse, image, precision=highest, preferred_element_type=F32)
        for k in range(2):
            mate_copy(k).wait_send()
        far_copy.wait_send()
        for kz in range(nz):
            pair_copy(kz).wait_send()
            (line_relay() if kz == 1 else pair_gather(kz)).wait_send()
        for kz in range(1, nz):
            line_copy(kz).wait_send()
            line_gather(kz).wait_send()
    for copy in waits:
        copy.wait_send()
    remote(s.band.at[1, 2], s.band.at[1, 3], s.band_send.at[3], s.band_recv.at[3], to(0, 1)).wait_send()


def scratch_of(nd, nb, slots, tile, k_vec, own_rows, own_cols):
    dma = pltpu.SemaphoreType.DMA
    row_tiles, col_tiles = own_rows * nb // tile, own_cols * nd // tile
    nz = nd // 2
    fold = (k_vec // 2, 2 * k_vec)
    buffers = {
        "tiles": ((slots, tile, tile), I32),
        "bits": ((slots + 1, tile, tile), BF16),
        "turned": ((slots + 1, tile, tile), BF16),
        "size_terms": ((slots + 1, 8, tile), F32),
        "doc_terms": ((slots + 1, 8, tile), F32),
        "table": ((8, tile), I32),
        "weight_terms": ((2, col_tiles, 16, tile), BF16),
        "degree_own": ((row_tiles, tile), F32),
        "degree": ((nb, row_tiles, tile), F32),
        "inv": ((row_tiles, tile), F32),
        "size": ((nd, 1, own_cols), F32),
        "size_from": ((nd, 1, own_cols), F32),
        "raw": ((nb, k_vec, own_rows), BF16),
        "band": ((ITERS, nb, k_vec, own_rows), BF16),
        "panel": ((nd, k_vec, own_cols), F32),
        "pair_out": ((ITERS, nz, k_vec, own_cols), BF16),
        "pair_in": ((ITERS, nz, k_vec, own_cols), BF16),
        "line_out": ((ITERS, nz, k_vec, own_cols), BF16),
        "line_in": ((ITERS, nz, k_vec, own_cols), BF16),
        "weighted": ((ITERS, nz, 2, k_vec, own_cols), BF16),
        "image": ((nb, k_vec, own_rows), F32),
        "mate_out": ((ITERS, 2, k_vec, own_rows), BF16),
        "mate_in": ((ITERS, 2, k_vec, own_rows), BF16),
        "far_out": ((ITERS, k_vec, own_rows), BF16),
        "far_in": ((ITERS, k_vec, own_rows), BF16),
        "gram_out": ((3,) + fold, F32),
        "gram_in": ((3,) + fold, F32),
        "gram_one": ((ITERS, 2 * nb) + fold, F32),
        "gram_two": ((ITERS, nz) + fold, F32),
    }
    total = 0
    for shape, kind in buffers.values():
        count = jnp.dtype(kind).itemsize
        for extent in shape:
            count *= extent
        total += count
    scratch = {name: pltpu.VMEM(shape, kind) for name, (shape, kind) in buffers.items()}
    scratch["slot"] = pltpu.SMEM((8, tile), I32)
    sems = {"load_sem": (CHUNKS,)}
    for name, shape in {
        "raw": (nb,),
        "deg": (nb,),
        "size": (nd,),
        "band": (nb,),
        "pair": (ITERS, nz),
        "line": (ITERS, nz),
        "wt": (ITERS, nz, 2),
        "mate": (ITERS, 2),
        "far": (ITERS,),
        "gs": (3,),
        "g1": (ITERS, 2 * nb),
        "g2": (ITERS, nz),
    }.items():
        sems[name + "_send"] = shape
        sems[name + "_recv"] = shape
    for name, shape in sems.items():
        scratch[name] = dma(shape)
    scratch["table_sem"] = dma
    return scratch, total


VMEM_BYTES = 60000 * 1024


def body(start_vectors, bucket_weight, tile_count, tile_coords, patterns):
    nd, nb = lax.axis_size("doc"), lax.axis_size("bkt")
    slots, tile = patterns.shape[2], patterns.shape[3]
    k_vec, own_rows = start_vectors.shape
    band_cols = bucket_weight.shape[0]
    own_cols = band_cols // nd
    scratch, total = scratch_of(nd, nb, slots, tile, k_vec, own_rows, own_cols)
    fits = total + 4 * k_vec * own_rows * 4 < VMEM_BYTES
    powers = nd & (nd - 1) == 0 and nd >= 4 and nb == 4
    whole = band_cols == nd * own_cols and own_cols == 2 * tile and 2 * k_vec == tile
    table = own_rows % (2 * tile) == 0 and own_rows // tile * (band_cols // tile) == tile and own_rows // tile % 8 == 0
    if not (fits and powers and whole and table and slots % (CHUNKS * GROUP) == 0):
        return plain_body(start_vectors, bucket_weight, tile_count, tile_coords, patterns)
    smem = pl.BlockSpec(memory_space=pltpu.SMEM)
    vmem = pl.BlockSpec(memory_space=pltpu.VMEM)
    anywhere = pl.BlockSpec(memory_space=pl.ANY)
    coords = tile_coords.reshape(slots, 2).T
    return pl.pallas_call(
        functools.partial(kernel, tuple(scratch), nd, nb),
        out_shape=jax.ShapeDtypeStruct((k_vec, own_rows), F32),
        in_specs=[smem, smem, vmem, vmem, vmem, anywhere],
        out_specs=vmem,
        scratch_shapes=list(scratch.values()),
        compiler_params=pltpu.CompilerParams(
            collective_id=0, has_side_effects=True, vmem_limit_bytes=VMEM_BYTES
        ),
        name="subspace",
    )(tile_count, coords, coords, start_vectors, bucket_weight.reshape(band_cols // tile, tile), patterns.reshape(slots, tile, tile))


def solution(mesh):
    in_specs = (
        P(None, ("doc", "bkt")),
        P("bkt"),
        P("doc", "bkt"),
        P("doc", "bkt", None, None),
        P("doc", "bkt", None, None, None),
    )
    out_specs = P(None, ("doc", "bkt"))
    return jax.shard_map(body, mesh=mesh, in_specs=in_specs, out_specs=out_specs, check_vma=False)
```

```python
import functools
import types

import jax
import jax.numpy as jnp
from jax import lax
from jax.experimental import pallas as pl
from jax.experimental.pallas import tpu as pltpu
from jax.sharding import PartitionSpec as P

ITERS = 2


def plain_body(start_vectors, bucket_weight, tile_count, tile_coords, patterns):
    highest = lax.Precision.HIGHEST
    slot_total = patterns.shape[2]
    tile_size = patterns.shape[3]
    vector_count = start_vectors.shape[0]
    own_rows = start_vectors.shape[1]
    band_rows = own_rows * lax.axis_size("bkt")
    band_cols = bucket_weight.shape[0]
    row_tiles = band_rows // tile_size
    col_tiles = band_cols // tile_size
    total_docs = band_rows * lax.axis_size("doc")
    live_slot = (jnp.arange(slot_total) < tile_count[0, 0]).astype(jnp.int32)
    pattern_int = patterns[0, 0] * live_slot[:, None, None]
    pattern = pattern_int.astype(jnp.bfloat16)
    row_index = tile_coords[0, 0, :, 0]
    col_index = tile_coords[0, 0, :, 1]
    row_pick = jnp.arange(row_tiles)[:, None] == row_index[None, :]
    col_pick = jnp.arange(col_tiles)[:, None] == col_index[None, :]
    row_pick_f = row_pick.astype(jnp.float32)
    row_pick_b = row_pick.astype(jnp.bfloat16)
    col_pick_f = col_pick.astype(jnp.float32)
    col_pick_b = col_pick.astype(jnp.bfloat16)
    pattern_f = pattern_int.astype(jnp.float32)
    weight_tiles = bucket_weight.reshape(col_tiles, tile_size)
    slot_weight = jnp.dot(col_pick_f.T, weight_tiles, precision=highest)
    row_part = jnp.einsum("tij,tj->ti", pattern_f, slot_weight, precision=highest)
    doc_part = jnp.dot(row_pick_f, row_part, precision=highest).reshape(band_rows)
    col_part = jnp.sum(pattern_f, axis=1)
    bucket_part = jnp.dot(col_pick_f, col_part, precision=highest).reshape(band_cols)
    doc_degree = lax.psum(doc_part, "bkt")
    bucket_size = lax.psum(bucket_part.astype(jnp.bfloat16), "doc").astype(jnp.float32)
    inv_band = 1.0 / jnp.sqrt(jnp.maximum(doc_degree, 1.0))
    inv_own = lax.dynamic_slice_in_dim(inv_band, lax.axis_index("bkt") * own_rows, own_rows)
    bucket_scale = bucket_weight / jnp.maximum(bucket_size, 1.0)
    vectors = start_vectors
    for sweep_index in range(ITERS):
        scaled = (vectors * inv_own[None, :]).astype(jnp.bfloat16)
        band_vecs = lax.all_gather(scaled, "bkt", axis=1, tiled=True)
        picked = jnp.einsum(
            "rt,kri->kti",
            row_pick_b,
            band_vecs.reshape(vector_count, row_tiles, tile_size),
            preferred_element_type=jnp.float32,
        ).astype(jnp.bfloat16)
        products = jnp.einsum("kti,tij->ktj", picked, pattern, preferred_element_type=jnp.float32)
        panel_part = (
            jnp.zeros((vector_count, col_tiles, tile_size), jnp.float32)
            .at[:, col_index, :]
            .add(products)
        )
        panel_part = panel_part.reshape(vector_count, band_cols)
        panel_whole = lax.psum(panel_part, "doc")
        weighted = (panel_whole * bucket_scale[None, :]).astype(jnp.bfloat16)
        spread = jnp.einsum(
            "ct,kcj->ktj",
            col_pick_b,
            weighted.reshape(vector_count, col_tiles, tile_size),
            preferred_element_type=jnp.float32,
        ).astype(jnp.bfloat16)
        returned = jnp.einsum("ktj,tij->kti", spread, pattern, preferred_element_type=jnp.float32)
        row_terms = (
            jnp.zeros((vector_count, row_tiles, tile_size), jnp.float32)
            .at[:, row_index, :]
            .add(returned)
        )
        row_terms = row_terms.reshape(vector_count, band_rows)
        rows_own = (
            lax.psum_scatter(row_terms, "bkt", scatter_dimension=1, tiled=True) * inv_own[None, :]
        )
        gram_local = jnp.dot(rows_own, rows_own.T, precision=highest)
        gram_matrix = lax.psum(gram_local, ("doc", "bkt")) / total_docs
        factor = jnp.linalg.cholesky(gram_matrix)
        vectors = lax.linalg.triangular_solve(factor, rows_own, left_side=True, lower=True)
    return vectors


MESH = pl.DeviceIdType.MESH
F32 = jnp.float32
BF16 = jnp.bfloat16
I32 = jnp.int32
NT = (((1,), (1,)), ((), ()))
BLOCK = 8
CHUNKS = 8
GROUP = 16


def flip(value, k, bits):
    out = 0
    for at in range(bits):
        unit = 1 << at
        bit = lax.rem(lax.div(value, unit), 2)
        want = (k >> at) & 1 if isinstance(k, int) else lax.rem(lax.div(k, unit), 2)
        out = out + unit * (bit + want - 2 * bit * want)
    return out


def inverse_factor(gram, k_vec):
    row_at = lax.broadcasted_iota(I32, (k_vec, k_vec), 0)
    col_at = lax.broadcasted_iota(I32, (k_vec, k_vec), 1)
    eye = (row_at == col_at).astype(F32)
    work = jnp.concatenate([gram, eye], axis=1)
    for at in range(0, k_vec, BLOCK):
        top = at // 8 * 8
        part = work[top:]
        below = lax.broadcasted_iota(I32, part.shape, 0)
        cols = [jnp.broadcast_to(part[:, at + m : at + m + 1], part.shape) for m in range(BLOCK)]
        for m in range(BLOCK):
            row = at - top + m
            factor = jnp.where(below > row, cols[m] * (1.0 / cols[m][row : row + 1]), 0.0)
            part = part - factor * part[row : row + 1]
            for n in range(m + 1, BLOCK):
                cols[n] = cols[n] - factor * cols[n][row : row + 1]
        work = jnp.concatenate([work[:top], part], axis=0) if top else part
    pivots = jnp.sum(work[:, :k_vec] * eye, axis=1, keepdims=True)
    return work[:, k_vec:] / jnp.sqrt(pivots)


def kernel(names, nd, nb, count_ref, coord_ref, place_ref, start_ref, weight_ref, patterns_hbm, out_ref, image_hbm, *refs):
    s = types.SimpleNamespace(**dict(zip(names, refs, strict=True)))
    highest = lax.Precision.HIGHEST
    me_d = lax.axis_index("doc")
    me_b = lax.axis_index("bkt")
    d_bits, b_bits = nd.bit_length() - 1, nb.bit_length() - 1
    slots, tile = patterns_hbm.shape[0], patterns_hbm.shape[1]
    k_vec, own_rows = start_ref.shape
    col_tiles = weight_ref.shape[0]
    col_per = col_tiles // nd
    row_per = own_rows // tile
    own_cols = col_per * tile
    half_per = row_per // 2
    half_rows = half_per * tile
    total_docs = own_rows * nb * nd
    nz = nd // 2

    def to(kd, kb):
        return {"doc": flip(me_d, kd, d_bits), "bkt": flip(me_b, kb, b_bits)}

    def remote(src, dst, ssem, rsem, peer):
        return pltpu.make_async_remote_copy(
            src_ref=src, dst_ref=dst, send_sem=ssem, recv_sem=rsem,
            device_id=peer, device_id_type=MESH,
        )

    def send(*args):
        copy = remote(*args)
        copy.start()
        return copy

    per_chunk = slots // CHUNKS

    def load(c):
        part = pl.ds(c * per_chunk, per_chunk)
        return pltpu.make_async_copy(patterns_hbm.at[part], s.tiles.at[part], s.load_sem.at[c])

    for c in range(CHUNKS):
        load(c).start()

    barrier = pltpu.get_barrier_semaphore()
    peers = [(kd, kb) for kd in range(nd) for kb in range(nb) if (kd < 2 or kb == 0) and kd + kb]
    for kd, kb in peers:
        pl.semaphore_signal(barrier, inc=1, device_id=to(kd, kb), device_id_type=MESH)

    lane = lax.broadcasted_iota(I32, (1, slots), 1)
    place = place_ref[0:1, :] * col_tiles + place_ref[1:2, :]
    place = jnp.where(lane < count_ref[0, 0], place, -1)
    across = jnp.transpose(jnp.broadcast_to(place, (tile, slots)))
    position = lax.broadcasted_iota(I32, (slots, tile), 1)
    slot_at = lax.broadcasted_iota(I32, (slots, tile), 0)
    for b in range(nb):
        found = jnp.max(jnp.where(across == position + b * tile, slot_at, -1), axis=0, keepdims=True)
        s.table[b : b + 1, :] = jnp.where(found >= 0, found, slots)
    tables = pltpu.make_async_copy(s.table, s.slot, s.table_sem)
    tables.start()
    s.bits[slots] = jnp.zeros((tile, tile), BF16)
    s.turned[slots] = jnp.zeros((tile, tile), BF16)
    s.size_terms[slots] = jnp.zeros((8, tile), F32)
    s.doc_terms[slots] = jnp.zeros((8, tile), F32)

    for c in range(col_tiles):
        left = weight_ref[c : c + 1, :]
        terms = []
        for _ in range(3):
            terms.append(left.astype(BF16).astype(F32))
            left = left - terms[-1]
        zeros = jnp.zeros((5, tile), F32)
        gap = jnp.zeros((8, tile), F32)
        eight = jnp.concatenate(terms + [zeros], axis=0)
        s.weight_terms[0, c] = jnp.concatenate([eight, gap], axis=0).astype(BF16)
        s.weight_terms[1, c] = jnp.concatenate([gap, eight], axis=0).astype(BF16)
    s.raw[0] = start_ref[...].astype(BF16)
    pl.semaphore_wait(barrier, len(peers))

    def gather_start(buf, ssem, rsem):
        return [
            send(buf.at[0], buf.at[k], ssem.at[k], rsem.at[k], to(0, k))
            for k in (2, 1)
        ]

    def gather_relay(buf, ssem, rsem, sent):
        sent[0].wait_recv()
        sent.append(send(buf.at[2], buf.at[3], ssem.at[3], rsem.at[3], to(0, 1)))

    waits = gather_start(s.raw, s.raw_send, s.raw_recv)
    raw_sent = waits


    def convert(c):
        load(c).wait()

        @pl.loop(0, per_chunk // GROUP)
        def _(g):
            base = c * per_chunk + g * GROUP
            for u in range(0, GROUP, 2):
                pair = []
                for v in range(2):
                    at = base + u + v
                    block = s.tiles[at].astype(F32)
                    s.size_terms[at] = jnp.sum(block.reshape(tile // 8, 8, tile), axis=0)
                    block = block.astype(BF16)
                    s.bits[at] = block
                    pair.append(jnp.transpose(block))
                    s.turned[at] = pair[v]
                left = jnp.concatenate(
                    [s.weight_terms[0, coord_ref[1, base + u]], s.weight_terms[1, coord_ref[1, base + u + 1]]], axis=1
                )
                sums = jnp.dot(left, jnp.concatenate(pair, axis=0), preferred_element_type=F32)
                s.doc_terms[base + u] = sums[:8]
                s.doc_terms[base + u + 1] = sums[8:]

    pl.loop(0, CHUNKS - 1)(convert)
    gather_relay(s.raw, s.raw_send, s.raw_recv, raw_sent)
    convert(CHUNKS - 1)
    tables.wait()

    def slot_of(b, i, c):
        return s.slot[b, i * col_tiles + c]

    for b in range(nb):
        for i in range(row_per):
            total = s.doc_terms[slot_of(b, i, 0)]
            for c in range(1, col_tiles):
                total = total + s.doc_terms[slot_of(b, i, c)]
            s.degree_own[b * row_per + i : b * row_per + i + 1, :] = total[0:1] + total[1:2] + total[2:3]
    s.degree[me_b] = s.degree_own[...]
    degree_sent = [
        send(s.degree.at[me_b], s.degree.at[me_b], s.deg_send.at[k], s.deg_recv.at[k], to(0, k))
        for k in range(nb - 1, 0, -1)
    ]
    for c in range(col_tiles):
        total = s.size_terms[slot_of(0, 0, c)]
        for b in range(nb):
            for i in range(0 if b else 1, row_per):
                total = total + s.size_terms[slot_of(b, i, c)]
        total = jnp.sum(total, axis=0, keepdims=True)
        s.size[c // col_per, :, c % col_per * tile : (c % col_per + 1) * tile] = total
    size_sent = []
    for k in range(nd - 1, 0, -1):
        size_sent.append(
            send(s.size.at[flip(me_d, k, d_bits)], s.size_from.at[k], s.size_send.at[k], s.size_recv.at[k], to(k, 0))
        )
    for copy in degree_sent:
        copy.wait()
    degree = s.degree[0]
    for b in range(1, nb):
        degree = degree + s.degree[b]
    s.inv[...] = 1.0 / jnp.sqrt(jnp.maximum(degree, 1.0))
    for copy in raw_sent[1:]:
        copy.wait_recv()
    for k in range(nb):
        first = flip(me_b, k, b_bits) * row_per
        inv_rows = s.inv[pl.ds(pl.multiple_of(first, row_per), row_per), :]
        for i in range(row_per):
            lanes = slice(i * tile, (i + 1) * tile)
            half_lanes = slice(i % half_per * tile, (i % half_per + 1) * tile)
            s.band[0, k, i // half_per, :, half_lanes] = (s.raw[k, :, lanes].astype(F32) * inv_rows[i : i + 1]).astype(BF16)
    inv_own = s.inv[pl.ds(pl.multiple_of(me_b * row_per, row_per), row_per), :]

    def tiles_of(b, i, o):
        pick = [[s.bits[slot_of(b, i + u, o * col_per + h)] for h in range(col_per)] for u in range(2)]
        return jnp.concatenate([jnp.concatenate(row, axis=1) for row in pick], axis=0)

    def panel_of(it, kd, sources, acc):
        o = flip(me_d, kd, d_bits)
        for k in sources:
            b = flip(me_b, k, b_bits)
            for i in range(0, row_per, 2):
                left = s.band[it, k, i // half_per, :, i % half_per * tile : (i % half_per + 2) * tile]
                term = jnp.dot(left, tiles_of(b, i, o), preferred_element_type=F32)
                acc = term if acc is None else acc + term
        return acc

    def image_of(q, left, o, first=0, last=row_per):
        rows = []
        for h in range(col_per):
            row = [s.turned[slot_of(q, i, o * col_per + h)] for i in range(first, last)]
            rows.append(jnp.concatenate(row, axis=1))
        return jnp.dot(left, jnp.concatenate(rows, axis=0), preferred_element_type=F32)

    def gram_of(image):
        high = image.astype(BF16)
        low = (image - high.astype(F32)).astype(BF16)
        both = jnp.concatenate([high, low], axis=0)
        gram = lax.dot_general(both, both, NT, preferred_element_type=F32)
        gram = gram[:k_vec] + gram[k_vec:]
        gram = gram[:, :k_vec] + gram[:, k_vec:]
        half = k_vec // 2
        return jnp.concatenate([gram[:half], gram[half:]], axis=1)

    steps = (to(0, 1), to(1, 0), to(0, 2))

    def gram_step(at, total):
        s.gram_out[at] = total
        return send(s.gram_out.at[at], s.gram_in.at[at], s.gs_send.at[at], s.gs_recv.at[at], steps[at])

    def gram_sum(at, copy):
        copy.wait_recv()
        return s.gram_out[at] + s.gram_in[at]

    def gram_start(it, image):
        mine = lax.rem(me_d, 2) * nb + me_b
        s.gram_one[it, mine] = gram_of(image)
        return [
            send(s.gram_one.at[it, mine], s.gram_one.at[it, mine], s.g1_send.at[it, k], s.g1_recv.at[it, k], to(k // nb, k % nb))
            for k in range(2 * nb - 1, 0, -1)
        ]

    def gram_middle(it, sent):
        for copy in sent:
            copy.wait_recv()
        total = s.gram_one[it, 0]
        for k in range(1, 2 * nb):
            total = total + s.gram_one[it, k]
        return gram_line(it, total)

    def gram_line(it, total):
        mine = lax.div(me_d, 2)
        s.gram_two[it, mine] = total
        return [
            send(s.gram_two.at[it, mine], s.gram_two.at[it, mine], s.g2_send.at[it, k], s.g2_recv.at[it, k], to(2 * k, 0))
            for k in range(nz - 1, 0, -1)
        ]

    def gram_end(it, sent):
        for copy in sent:
            copy.wait_recv()
        total = s.gram_two[it, 0]
        for k in range(1, nz):
            total = total + s.gram_two[it, k]
        return jnp.concatenate([total[:, :k_vec], total[:, k_vec:]], axis=0) / total_docs

    def band_copy(k, h):
        if k == 3:
            src, peer = s.band.at[1, 2, h], to(0, 1)
        else:
            src, peer = s.band.at[1, 0, h], to(0, k)
        return remote(src, s.band.at[1, k, h], s.band_send.at[k, h], s.band_recv.at[k, h], peer)

    waits = list(raw_sent)
    inverse = None
    for it in range(ITERS):
        first = it == 0

        def pair_copy(kz):
            return remote(
                s.pair_out.at[it, kz], s.pair_in.at[it, kz], s.pair_send.at[it, kz], s.pair_recv.at[it, kz], to(1, 0)
            )

        def line_copy(kz):
            return remote(
                s.line_out.at[it, kz], s.line_in.at[it, kz], s.line_send.at[it, kz], s.line_recv.at[it, kz], to(2 * kz, 0)
            )

        if not first:

            for kd in range(nd):
                s.panel[kd] = panel_of(it, kd, (0,), None)

            gram_copies = [gram_sent, gram_step(1, gram_sum(0, gram_sent))]
            for h in range(2):
                band_copy(1, h).wait_recv()

            for kd in range(nd):
                s.panel[kd] = panel_of(it, kd, (1,), s.panel[kd])

            band_copy(2, 0).wait_recv()
            band_copy(3, 0).start()
            gram_copies.append(gram_step(2, gram_sum(1, gram_copies[1])))
            band_copy(2, 1).wait_recv()
            band_copy(3, 1).start()

            for kd in range(nd):
                s.panel[kd] = panel_of(it, kd, (2,), s.panel[kd])

            for h in range(2):
                band_copy(3, h).wait_recv()

        sources = tuple(range(nb)) if first else (nb - 1,)


        @pl.loop(0, nz)
        def _(at):
            kz = nz - 1 - at
            kd = 2 * kz + 1
            total = panel_of(it, kd, sources, None if first else s.panel[kd])
            s.pair_out[it, kz] = total.astype(BF16)
            pair_copy(kz).start()

        if not first:
            gram_sent_two = gram_line(it - 1, gram_sum(2, gram_copies[2]))
            waits += gram_copies

        @pl.loop(0, nz - 1)
        def _(at):
            kz = nz - 1 - at
            kd = 2 * kz
            total = panel_of(it, kd, sources, None if first else s.panel[kd])
            pair_copy(kz).wait_recv()
            s.line_out[it, kz] = (total + s.pair_in[it, kz].astype(F32)).astype(BF16)
            line_copy(kz).start()

        whole = panel_of(it, 0, sources, None if first else s.panel[0])
        if not first:
            gram = gram_end(it - 1, gram_sent_two)
            inverse = inverse_factor(gram, k_vec)
            waits += gram_sent_two
        pair_copy(0).wait_recv()
        whole = whole + s.pair_in[it, 0].astype(F32)
        for kz in range(1, nz):
            line_copy(kz).wait_recv()
            whole = whole + s.line_in[it, kz].astype(F32)
        if first:
            for copy in size_sent:
                copy.wait()
            size = s.size[me_d]
            for k in range(1, nd):
                size = size + s.size_from[k]
            weight_own = jnp.concatenate([weight_ref[pl.ds(me_d * col_per + h, 1), :] for h in range(col_per)], axis=1)
            scale = weight_own / jnp.maximum(size, 1.0)
        else:
            whole = jnp.dot(inverse, whole, precision=highest, preferred_element_type=F32)
        s.weighted[it, 0, 0] = (whole * scale).astype(BF16)

        def line_gather(kz):
            return remote(
                s.weighted.at[it, 0, 0], s.weighted.at[it, kz, 0], s.wt_send.at[it, kz, 0], s.wt_recv.at[it, kz, 0], to(2 * kz, 0)
            )

        def pair_gather(kz):
            return remote(
                s.weighted.at[it, kz, 0], s.weighted.at[it, kz, 1], s.wt_send.at[it, kz, 1], s.wt_recv.at[it, kz, 1], to(1, 0)
            )

        for kz in range(nz - 1, 0, -1):
            line_gather(kz).start()
        pair_gather(0).start()

        def source(kz, side):
            return flip(me_d, 2 * kz + side, d_bits)

        def line_relay():
            return remote(
                s.weighted.at[it, 0, 1], s.weighted.at[it, 1, 1], s.wt_send.at[it, 1, 1], s.wt_recv.at[it, 1, 1], to(2, 0)
            )

        def add_block(kz, side, fresh=False):
            for q in range(nb):
                term = image_of(q, s.weighted[it, kz, side], source(kz, side))
                s.image[q] = term if fresh else s.image[q] + term

        add_block(0, 0, True)
        pair_gather(0).wait_recv()
        line_relay().start()
        add_block(0, 1)
        line_gather(1).wait_recv()
        add_block(1, 0)

        @pl.loop(2, nz)
        def _(kz):
            line_gather(kz).wait_recv()
            pair_gather(kz).start()
            add_block(kz, 0)

        line_relay().wait_recv()
        add_block(1, 1)

        @pl.loop(2, nz - 1)
        def _(kz):
            pair_gather(kz).wait_recv()
            add_block(kz, 1)

        pair_gather(nz - 1).wait_recv()

        def finish(k, h):
            q = flip(me_b, k, b_bits)
            term = image_of(q, s.weighted[it, nz - 1, 1], source(nz - 1, 1), h * half_per, (h + 1) * half_per)
            return s.image[q, :, h * half_rows : (h + 1) * half_rows] + term

        def mate_copy(k, h):
            return remote(
                s.mate_out.at[it, k, h], s.mate_in.at[it, k, h], s.mate_send.at[it, k, h], s.mate_recv.at[it, k, h], to(0, 1)
            )

        def far_copy(h):
            return remote(s.far_out.at[it, h], s.far_in.at[it, h], s.far_send.at[it, h], s.far_recv.at[it, h], to(0, 2))

        def weigh(value, h):
            parts = [
                value[:, i * tile : (i + 1) * tile] * inv_own[h * half_per + i : h * half_per + i + 1]
                for i in range(half_per)
            ]
            return jnp.concatenate(parts, axis=1)

        for h in range(2):
            s.mate_out[it, 1, h] = finish(3, h).astype(BF16)
            mate_copy(1, h).start()
        for h in range(2):
            both = finish(2, h)
            mate_copy(1, h).wait_recv()
            s.far_out[it, h] = (both + s.mate_in[it, 1, h].astype(F32)).astype(BF16)
            far_copy(h).start()
        for h in range(2):
            s.mate_out[it, 0, h] = finish(1, h).astype(BF16)
            mate_copy(0, h).start()
        halves = [finish(0, h) for h in range(2)]
        more = it + 1 < ITERS
        for h in range(2):
            mate_copy(0, h).wait_recv()
            far_copy(h).wait_recv()
            halves[h] = weigh(halves[h] + s.mate_in[it, 0, h].astype(F32) + s.far_in[it, h].astype(F32), h)
            if more:
                s.band[it + 1, 0, h] = weigh(halves[h], h).astype(BF16)
                for k in (2, 1):
                    band_copy(k, h).start()
        image = jnp.concatenate(halves, axis=1)
        if more:
            gram_sent = gram_step(0, gram_of(image))
        else:
            s.final[...] = image
            store = pltpu.make_async_copy(s.final, image_hbm, s.store_sem)
            store.start()
            gram_sent = gram_start(it, image)
            waits += gram_sent
            gram_sent_two = gram_middle(it, gram_sent)
            waits += gram_sent_two
            gram = gram_end(it, gram_sent_two)
            inverse = inverse_factor(gram, k_vec)
            out_ref[...] = inverse
            store.wait()
        for h in range(2):
            for k in range(2):
                mate_copy(k, h).wait_send()
            far_copy(h).wait_send()
        for kz in range(nz):
            pair_copy(kz).wait_send()
            (line_relay() if kz == 1 else pair_gather(kz)).wait_send()
        for kz in range(1, nz):
            line_copy(kz).wait_send()
            line_gather(kz).wait_send()
    for copy in waits:
        copy.wait_send()
    for k in range(1, nb):
        for h in range(2):
            band_copy(k, h).wait_send()


def scratch_of(nd, nb, slots, tile, k_vec, own_rows, own_cols):
    dma = pltpu.SemaphoreType.DMA
    row_tiles, col_tiles = own_rows * nb // tile, own_cols * nd // tile
    nz = nd // 2
    fold = (k_vec // 2, 2 * k_vec)
    buffers = {
        "tiles": ((slots, tile, tile), I32),
        "bits": ((slots + 1, tile, tile), BF16),
        "turned": ((slots + 1, tile, tile), BF16),
        "size_terms": ((slots + 1, 8, tile), F32),
        "doc_terms": ((slots + 1, 8, tile), F32),
        "table": ((8, tile), I32),
        "weight_terms": ((2, col_tiles, 16, tile), BF16),
        "degree_own": ((row_tiles, tile), F32),
        "degree": ((nb, row_tiles, tile), F32),
        "inv": ((row_tiles, tile), F32),
        "size": ((nd, 1, own_cols), F32),
        "size_from": ((nd, 1, own_cols), F32),
        "raw": ((nb, k_vec, own_rows), BF16),
        "band": ((ITERS, nb, 2, k_vec, own_rows // 2), BF16),
        "panel": ((nd, k_vec, own_cols), F32),
        "pair_out": ((ITERS, nz, k_vec, own_cols), BF16),
        "pair_in": ((ITERS, nz, k_vec, own_cols), BF16),
        "line_out": ((ITERS, nz, k_vec, own_cols), BF16),
        "line_in": ((ITERS, nz, k_vec, own_cols), BF16),
        "weighted": ((ITERS, nz, 2, k_vec, own_cols), BF16),
        "image": ((nb, k_vec, own_rows), F32),
        "mate_out": ((ITERS, 2, 2, k_vec, own_rows // 2), BF16),
        "mate_in": ((ITERS, 2, 2, k_vec, own_rows // 2), BF16),
        "far_out": ((ITERS, 2, k_vec, own_rows // 2), BF16),
        "far_in": ((ITERS, 2, k_vec, own_rows // 2), BF16),
        "final": ((k_vec, own_rows), F32),
        "gram_out": ((3,) + fold, F32),
        "gram_in": ((3,) + fold, F32),
        "gram_one": ((ITERS, 2 * nb) + fold, F32),
        "gram_two": ((ITERS, nz) + fold, F32),
    }
    total = 0
    for shape, kind in buffers.values():
        count = jnp.dtype(kind).itemsize
        for extent in shape:
            count *= extent
        total += count
    scratch = {name: pltpu.VMEM(shape, kind) for name, (shape, kind) in buffers.items()}
    scratch["slot"] = pltpu.SMEM((8, tile), I32)
    sems = {"load_sem": (CHUNKS,)}
    for name, shape in {
        "raw": (nb,),
        "deg": (nb,),
        "size": (nd,),
        "band": (nb, 2),
        "pair": (ITERS, nz),
        "line": (ITERS, nz),
        "wt": (ITERS, nz, 2),
        "mate": (ITERS, 2, 2),
        "far": (ITERS, 2),
        "gs": (3,),
        "g1": (ITERS, 2 * nb),
        "g2": (ITERS, nz),
    }.items():
        sems[name + "_send"] = shape
        sems[name + "_recv"] = shape
    for name, shape in sems.items():
        scratch[name] = dma(shape)
    scratch["table_sem"] = dma
    scratch["store_sem"] = dma
    return scratch, total


VMEM_BYTES = 60000 * 1024


def body(start_vectors, bucket_weight, tile_count, tile_coords, patterns):
    nd, nb = lax.axis_size("doc"), lax.axis_size("bkt")
    slots, tile = patterns.shape[2], patterns.shape[3]
    k_vec, own_rows = start_vectors.shape
    band_cols = bucket_weight.shape[0]
    own_cols = band_cols // nd
    scratch, total = scratch_of(nd, nb, slots, tile, k_vec, own_rows, own_cols)
    fits = total + 4 * k_vec * own_rows * 4 < VMEM_BYTES
    powers = nd & (nd - 1) == 0 and nd >= 4 and nb == 4
    whole = band_cols == nd * own_cols and own_cols == 2 * tile and 2 * k_vec == tile
    table = own_rows % (2 * tile) == 0 and own_rows // tile * (band_cols // tile) == tile and own_rows // tile % 8 == 0
    if not (fits and powers and whole and table and slots % (CHUNKS * GROUP) == 0):
        return plain_body(start_vectors, bucket_weight, tile_count, tile_coords, patterns)
    smem = pl.BlockSpec(memory_space=pltpu.SMEM)
    vmem = pl.BlockSpec(memory_space=pltpu.VMEM)
    anywhere = pl.BlockSpec(memory_space=pl.ANY)
    coords = tile_coords.reshape(slots, 2).T
    inverse, image = pl.pallas_call(
        functools.partial(kernel, tuple(scratch), nd, nb),
        out_shape=[jax.ShapeDtypeStruct((k_vec, k_vec), F32), jax.ShapeDtypeStruct((k_vec, own_rows), F32)],
        in_specs=[smem, smem, vmem, vmem, vmem, anywhere],
        out_specs=[vmem, anywhere],
        scratch_shapes=list(scratch.values()),
        compiler_params=pltpu.CompilerParams(
            collective_id=0, has_side_effects=True, vmem_limit_bytes=VMEM_BYTES
        ),
        name="subspace",
    )(tile_count, coords, coords, start_vectors, bucket_weight.reshape(band_cols // tile, tile), patterns.reshape(slots, tile, tile))
    return jnp.dot(inverse, image, precision=lax.Precision.HIGH)


def solution(mesh):
    in_specs = (
        P(None, ("doc", "bkt")),
        P("bkt"),
        P("doc", "bkt"),
        P("doc", "bkt", None, None),
        P("doc", "bkt", None, None, None),
    )
    out_specs = P(None, ("doc", "bkt"))
    return jax.shard_map(body, mesh=mesh, in_specs=in_specs, out_specs=out_specs, check_vma=False)
```

```python
import functools
import types

import jax
import jax.numpy as jnp
from jax import lax
from jax.experimental import pallas as pl
from jax.experimental.pallas import tpu as pltpu
from jax.sharding import PartitionSpec as P

ITERS = 2


def plain_body(start_vectors, bucket_weight, tile_count, tile_coords, patterns):
    highest = lax.Precision.HIGHEST
    slot_total = patterns.shape[2]
    tile_size = patterns.shape[3]
    vector_count = start_vectors.shape[0]
    own_rows = start_vectors.shape[1]
    band_rows = own_rows * lax.axis_size("bkt")
    band_cols = bucket_weight.shape[0]
    row_tiles = band_rows // tile_size
    col_tiles = band_cols // tile_size
    total_docs = band_rows * lax.axis_size("doc")
    live_slot = (jnp.arange(slot_total) < tile_count[0, 0]).astype(jnp.int32)
    pattern_int = patterns[0, 0] * live_slot[:, None, None]
    pattern = pattern_int.astype(jnp.bfloat16)
    row_index = tile_coords[0, 0, :, 0]
    col_index = tile_coords[0, 0, :, 1]
    row_pick = jnp.arange(row_tiles)[:, None] == row_index[None, :]
    col_pick = jnp.arange(col_tiles)[:, None] == col_index[None, :]
    row_pick_f = row_pick.astype(jnp.float32)
    row_pick_b = row_pick.astype(jnp.bfloat16)
    col_pick_f = col_pick.astype(jnp.float32)
    col_pick_b = col_pick.astype(jnp.bfloat16)
    pattern_f = pattern_int.astype(jnp.float32)
    weight_tiles = bucket_weight.reshape(col_tiles, tile_size)
    slot_weight = jnp.dot(col_pick_f.T, weight_tiles, precision=highest)
    row_part = jnp.einsum("tij,tj->ti", pattern_f, slot_weight, precision=highest)
    doc_part = jnp.dot(row_pick_f, row_part, precision=highest).reshape(band_rows)
    col_part = jnp.sum(pattern_f, axis=1)
    bucket_part = jnp.dot(col_pick_f, col_part, precision=highest).reshape(band_cols)
    doc_degree = lax.psum(doc_part, "bkt")
    bucket_size = lax.psum(bucket_part.astype(jnp.bfloat16), "doc").astype(jnp.float32)
    inv_band = 1.0 / jnp.sqrt(jnp.maximum(doc_degree, 1.0))
    inv_own = lax.dynamic_slice_in_dim(inv_band, lax.axis_index("bkt") * own_rows, own_rows)
    bucket_scale = bucket_weight / jnp.maximum(bucket_size, 1.0)
    vectors = start_vectors
    for sweep_index in range(ITERS):
        scaled = (vectors * inv_own[None, :]).astype(jnp.bfloat16)
        band_vecs = lax.all_gather(scaled, "bkt", axis=1, tiled=True)
        picked = jnp.einsum(
            "rt,kri->kti",
            row_pick_b,
            band_vecs.reshape(vector_count, row_tiles, tile_size),
            preferred_element_type=jnp.float32,
        ).astype(jnp.bfloat16)
        products = jnp.einsum("kti,tij->ktj", picked, pattern, preferred_element_type=jnp.float32)
        panel_part = (
            jnp.zeros((vector_count, col_tiles, tile_size), jnp.float32)
            .at[:, col_index, :]
            .add(products)
        )
        panel_part = panel_part.reshape(vector_count, band_cols)
        panel_whole = lax.psum(panel_part, "doc")
        weighted = (panel_whole * bucket_scale[None, :]).astype(jnp.bfloat16)
        spread = jnp.einsum(
            "ct,kcj->ktj",
            col_pick_b,
            weighted.reshape(vector_count, col_tiles, tile_size),
            preferred_element_type=jnp.float32,
        ).astype(jnp.bfloat16)
        returned = jnp.einsum("ktj,tij->kti", spread, pattern, preferred_element_type=jnp.float32)
        row_terms = (
            jnp.zeros((vector_count, row_tiles, tile_size), jnp.float32)
            .at[:, row_index, :]
            .add(returned)
        )
        row_terms = row_terms.reshape(vector_count, band_rows)
        rows_own = (
            lax.psum_scatter(row_terms, "bkt", scatter_dimension=1, tiled=True) * inv_own[None, :]
        )
        gram_local = jnp.dot(rows_own, rows_own.T, precision=highest)
        gram_matrix = lax.psum(gram_local, ("doc", "bkt")) / total_docs
        factor = jnp.linalg.cholesky(gram_matrix)
        vectors = lax.linalg.triangular_solve(factor, rows_own, left_side=True, lower=True)
    return vectors


MESH = pl.DeviceIdType.MESH
F32 = jnp.float32
BF16 = jnp.bfloat16
I32 = jnp.int32
NT = (((1,), (1,)), ((), ()))
BLOCK = 16
CHUNKS = 8
GROUP = 16


def flip(value, k, bits):
    out = 0
    for at in range(bits):
        unit = 1 << at
        bit = lax.rem(lax.div(value, unit), 2)
        want = (k >> at) & 1 if isinstance(k, int) else lax.rem(lax.div(k, unit), 2)
        out = out + unit * (bit + want - 2 * bit * want)
    return out


def inverse_factor(gram, k_vec):
    row_at = lax.broadcasted_iota(I32, (k_vec, k_vec), 0)
    col_at = lax.broadcasted_iota(I32, (k_vec, k_vec), 1)
    eye = (row_at == col_at).astype(F32)
    work = jnp.concatenate([gram, eye], axis=1)
    for at in range(0, k_vec, BLOCK):
        top = at // 8 * 8
        part = work[top:]
        below = lax.broadcasted_iota(I32, part.shape, 0)
        cols = [jnp.broadcast_to(part[:, at + m : at + m + 1], part.shape) for m in range(BLOCK)]
        for m in range(BLOCK):
            row = at - top + m
            factor = jnp.where(below > row, cols[m] * (1.0 / cols[m][row : row + 1]), 0.0)
            part = part - factor * part[row : row + 1]
            for n in range(m + 1, BLOCK):
                cols[n] = cols[n] - factor * cols[n][row : row + 1]
        work = jnp.concatenate([work[:top], part], axis=0) if top else part
    pivots = jnp.sum(work[:, :k_vec] * eye, axis=1, keepdims=True)
    return work[:, k_vec:] / jnp.sqrt(pivots)


def kernel(names, nd, nb, count_ref, coord_ref, place_ref, start_ref, weight_ref, patterns_hbm, out_ref, image_hbm, *refs):
    s = types.SimpleNamespace(**dict(zip(names, refs, strict=True)))
    highest = lax.Precision.HIGHEST
    me_d = lax.axis_index("doc")
    me_b = lax.axis_index("bkt")
    d_bits, b_bits = nd.bit_length() - 1, nb.bit_length() - 1
    slots, tile = patterns_hbm.shape[0], patterns_hbm.shape[1]
    k_vec, own_rows = start_ref.shape
    col_tiles = weight_ref.shape[0]
    col_per = col_tiles // nd
    row_per = own_rows // tile
    own_cols = col_per * tile
    half_per = row_per // 2
    half_rows = half_per * tile
    total_docs = own_rows * nb * nd
    nz = nd // 2

    def to(kd, kb):
        return {"doc": flip(me_d, kd, d_bits), "bkt": flip(me_b, kb, b_bits)}

    def remote(src, dst, ssem, rsem, peer):
        return pltpu.make_async_remote_copy(
            src_ref=src, dst_ref=dst, send_sem=ssem, recv_sem=rsem,
            device_id=peer, device_id_type=MESH,
        )

    def send(*args):
        copy = remote(*args)
        copy.start()
        return copy

    per_chunk = slots // CHUNKS

    def load(c):
        part = pl.ds(c * per_chunk, per_chunk)
        return pltpu.make_async_copy(patterns_hbm.at[part], s.tiles.at[part], s.load_sem.at[c])

    for c in range(CHUNKS):
        load(c).start()

    barrier = pltpu.get_barrier_semaphore()
    peers = [(kd, kb) for kd in range(nd) for kb in range(nb) if (kd < 2 or kb == 0) and kd + kb]
    for kd, kb in peers:
        pl.semaphore_signal(barrier, inc=1, device_id=to(kd, kb), device_id_type=MESH)

    lane = lax.broadcasted_iota(I32, (1, slots), 1)
    place = place_ref[0:1, :] * col_tiles + place_ref[1:2, :]
    place = jnp.where(lane < count_ref[0, 0], place, -1)
    across = jnp.transpose(jnp.broadcast_to(place, (tile, slots)))
    position = lax.broadcasted_iota(I32, (slots, tile), 1)
    slot_at = lax.broadcasted_iota(I32, (slots, tile), 0)
    for b in range(nb):
        found = jnp.max(jnp.where(across == position + b * tile, slot_at, -1), axis=0, keepdims=True)
        s.table[b : b + 1, :] = jnp.where(found >= 0, found, slots)
    tables = pltpu.make_async_copy(s.table, s.slot, s.table_sem)
    tables.start()
    s.bits[slots] = jnp.zeros((tile, tile), BF16)
    s.turned[slots] = jnp.zeros((tile, tile), BF16)
    s.size_terms[slots] = jnp.zeros((8, tile), F32)
    s.doc_terms[slots] = jnp.zeros((8, tile), F32)

    for c in range(col_tiles):
        left = weight_ref[c : c + 1, :]
        terms = []
        for _ in range(3):
            terms.append(left.astype(BF16).astype(F32))
            left = left - terms[-1]
        zeros = jnp.zeros((5, tile), F32)
        gap = jnp.zeros((8, tile), F32)
        eight = jnp.concatenate(terms + [zeros], axis=0)
        s.weight_terms[0, c] = jnp.concatenate([eight, gap], axis=0).astype(BF16)
        s.weight_terms[1, c] = jnp.concatenate([gap, eight], axis=0).astype(BF16)
    s.raw[0] = start_ref[...].astype(BF16)
    pl.semaphore_wait(barrier, len(peers))

    def gather_start(buf, ssem, rsem):
        return [
            send(buf.at[0], buf.at[k], ssem.at[k], rsem.at[k], to(0, k))
            for k in (2, 1)
        ]

    def gather_relay(buf, ssem, rsem, sent):
        sent[0].wait_recv()
        sent.append(send(buf.at[2], buf.at[3], ssem.at[3], rsem.at[3], to(0, 1)))

    waits = gather_start(s.raw, s.raw_send, s.raw_recv)
    raw_sent = waits


    def convert(c):
        load(c).wait()

        @pl.loop(0, per_chunk // GROUP)
        def _(g):
            base = c * per_chunk + g * GROUP
            for u in range(0, GROUP, 2):
                pair = []
                for v in range(2):
                    at = base + u + v
                    block = s.tiles[at].astype(F32)
                    s.size_terms[at] = jnp.sum(block.reshape(tile // 8, 8, tile), axis=0)
                    block = block.astype(BF16)
                    s.bits[at] = block
                    pair.append(jnp.transpose(block))
                    s.turned[at] = pair[v]
                left = jnp.concatenate(
                    [s.weight_terms[0, coord_ref[1, base + u]], s.weight_terms[1, coord_ref[1, base + u + 1]]], axis=1
                )
                sums = jnp.dot(left, jnp.concatenate(pair, axis=0), preferred_element_type=F32)
                s.doc_terms[base + u] = sums[:8]
                s.doc_terms[base + u + 1] = sums[8:]

    pl.loop(0, CHUNKS - 1)(convert)
    gather_relay(s.raw, s.raw_send, s.raw_recv, raw_sent)
    convert(CHUNKS - 1)
    tables.wait()

    def slot_of(b, i, c):
        return s.slot[b, i * col_tiles + c]

    for b in range(nb):
        for i in range(row_per):
            total = s.doc_terms[slot_of(b, i, 0)]
            for c in range(1, col_tiles):
                total = total + s.doc_terms[slot_of(b, i, c)]
            s.degree_own[b * row_per + i : b * row_per + i + 1, :] = total[0:1] + total[1:2] + total[2:3]
    s.degree[me_b] = s.degree_own[...]
    degree_sent = [
        send(s.degree.at[me_b], s.degree.at[me_b], s.deg_send.at[k], s.deg_recv.at[k], to(0, k))
        for k in range(nb - 1, 0, -1)
    ]
    for c in range(col_tiles):
        total = s.size_terms[slot_of(0, 0, c)]
        for b in range(nb):
            for i in range(0 if b else 1, row_per):
                total = total + s.size_terms[slot_of(b, i, c)]
        total = jnp.sum(total, axis=0, keepdims=True)
        s.size[c // col_per, :, c % col_per * tile : (c % col_per + 1) * tile] = total
    size_sent = []
    for k in range(nd - 1, 0, -1):
        size_sent.append(
            send(s.size.at[flip(me_d, k, d_bits)], s.size_from.at[k], s.size_send.at[k], s.size_recv.at[k], to(k, 0))
        )
    for copy in degree_sent:
        copy.wait()
    degree = s.degree[0]
    for b in range(1, nb):
        degree = degree + s.degree[b]
    s.inv[...] = 1.0 / jnp.sqrt(jnp.maximum(degree, 1.0))
    for copy in raw_sent[1:]:
        copy.wait_recv()
    for k in range(nb):
        first = flip(me_b, k, b_bits) * row_per
        inv_rows = s.inv[pl.ds(pl.multiple_of(first, row_per), row_per), :]
        for i in range(row_per):
            lanes = slice(i * tile, (i + 1) * tile)
            half_lanes = slice(i % half_per * tile, (i % half_per + 1) * tile)
            s.band[0, k, i // half_per, :, half_lanes] = (s.raw[k, :, lanes].astype(F32) * inv_rows[i : i + 1]).astype(BF16)
    inv_own = s.inv[pl.ds(pl.multiple_of(me_b * row_per, row_per), row_per), :]

    def tiles_of(b, i, o):
        pick = [[s.bits[slot_of(b, i + u, o * col_per + h)] for h in range(col_per)] for u in range(2)]
        return jnp.concatenate([jnp.concatenate(row, axis=1) for row in pick], axis=0)

    def panel_of(it, kd, sources, acc):
        o = flip(me_d, kd, d_bits)
        for k in sources:
            b = flip(me_b, k, b_bits)
            for i in range(0, row_per, 2):
                left = s.band[it, k, i // half_per, :, i % half_per * tile : (i % half_per + 2) * tile]
                term = jnp.dot(left, tiles_of(b, i, o), preferred_element_type=F32)
                acc = term if acc is None else acc + term
        return acc

    def image_of(q, left, o, first=0, last=row_per):
        rows = []
        for h in range(col_per):
            row = [s.turned[slot_of(q, i, o * col_per + h)] for i in range(first, last)]
            rows.append(jnp.concatenate(row, axis=1))
        return jnp.dot(left, jnp.concatenate(rows, axis=0), preferred_element_type=F32)

    def gram_part(image):
        high = image.astype(BF16)
        low = (image - high.astype(F32)).astype(BF16)
        both = jnp.concatenate([high, low], axis=0)
        return lax.dot_general(both, both, NT, preferred_element_type=F32)

    def gram_of(gram):
        gram = gram[:k_vec] + gram[k_vec:]
        gram = gram[:, :k_vec] + gram[:, k_vec:]
        half = k_vec // 2
        return jnp.concatenate([gram[:half], gram[half:]], axis=1)

    steps = (to(0, 1), to(1, 0), to(0, 2))

    def gram_step(at, total):
        s.gram_out[at] = total
        return send(s.gram_out.at[at], s.gram_in.at[at], s.gs_send.at[at], s.gs_recv.at[at], steps[at])

    def gram_sum(at, copy):
        copy.wait_recv()
        return s.gram_out[at] + s.gram_in[at]

    def gram_start(it, gram):
        mine = lax.rem(me_d, 2) * nb + me_b
        s.gram_one[it, mine] = gram_of(gram)
        return [
            send(s.gram_one.at[it, mine], s.gram_one.at[it, mine], s.g1_send.at[it, k], s.g1_recv.at[it, k], to(k // nb, k % nb))
            for k in range(2 * nb - 1, 0, -1)
        ]

    def gram_middle(it, sent):
        for copy in sent:
            copy.wait_recv()
        total = s.gram_one[it, 0]
        for k in range(1, 2 * nb):
            total = total + s.gram_one[it, k]
        return gram_line(it, total)

    def gram_line(it, total):
        mine = lax.div(me_d, 2)
        s.gram_two[it, mine] = total
        return [
            send(s.gram_two.at[it, mine], s.gram_two.at[it, mine], s.g2_send.at[it, k], s.g2_recv.at[it, k], to(2 * k, 0))
            for k in range(nz - 1, 0, -1)
        ]

    def gram_end(it, sent):
        for copy in sent:
            copy.wait_recv()
        total = s.gram_two[it, 0]
        for k in range(1, nz):
            total = total + s.gram_two[it, k]
        return jnp.concatenate([total[:, :k_vec], total[:, k_vec:]], axis=0) / total_docs

    def band_copy(k, h):
        if k == 3:
            src, peer = s.band.at[1, 2, h], to(0, 1)
        else:
            src, peer = s.band.at[1, 0, h], to(0, k)
        return remote(src, s.band.at[1, k, h], s.band_send.at[k, h], s.band_recv.at[k, h], peer)

    waits = list(raw_sent)
    inverse = None
    for it in range(ITERS):
        first = it == 0

        def pair_copy(kz):
            return remote(
                s.pair_out.at[it, kz], s.pair_in.at[it, kz], s.pair_send.at[it, kz], s.pair_recv.at[it, kz], to(1, 0)
            )

        def line_copy(kz):
            return remote(
                s.line_out.at[it, kz], s.line_in.at[it, kz], s.line_send.at[it, kz], s.line_recv.at[it, kz], to(2 * kz, 0)
            )

        if not first:

            for kd in range(nd):
                s.panel[kd] = panel_of(it, kd, (0,), None)

            gram_copies = [gram_sent, gram_step(1, gram_sum(0, gram_sent))]
            for h in range(2):
                band_copy(1, h).wait_recv()

            for kd in range(nd):
                s.panel[kd] = panel_of(it, kd, (1,), s.panel[kd])

            band_copy(2, 0).wait_recv()
            band_copy(3, 0).start()
            gram_copies.append(gram_step(2, gram_sum(1, gram_copies[1])))
            band_copy(2, 1).wait_recv()
            band_copy(3, 1).start()

            for kd in range(nd):
                s.panel[kd] = panel_of(it, kd, (2,), s.panel[kd])

            for h in range(2):
                band_copy(3, h).wait_recv()

        sources = tuple(range(nb)) if first else (nb - 1,)


        @pl.loop(0, nz)
        def _(at):
            kz = nz - 1 - at
            kd = 2 * kz + 1
            total = panel_of(it, kd, sources, None if first else s.panel[kd])
            s.pair_out[it, kz] = total.astype(BF16)
            pair_copy(kz).start()

        if not first:
            gram_sent_two = gram_line(it - 1, gram_sum(2, gram_copies[2]))
            waits += gram_copies

        @pl.loop(0, nz - 1)
        def _(at):
            kz = nz - 1 - at
            kd = 2 * kz
            total = panel_of(it, kd, sources, None if first else s.panel[kd])
            pair_copy(kz).wait_recv()
            s.line_out[it, kz] = (total + s.pair_in[it, kz].astype(F32)).astype(BF16)
            line_copy(kz).start()

        whole = panel_of(it, 0, sources, None if first else s.panel[0])
        if not first:
            gram = gram_end(it - 1, gram_sent_two)
            inverse = inverse_factor(gram, k_vec)
            waits += gram_sent_two
        pair_copy(0).wait_recv()
        whole = whole + s.pair_in[it, 0].astype(F32)
        for kz in range(1, nz):
            line_copy(kz).wait_recv()
            whole = whole + s.line_in[it, kz].astype(F32)
        if first:
            for copy in size_sent:
                copy.wait()
            size = s.size[me_d]
            for k in range(1, nd):
                size = size + s.size_from[k]
            weight_own = jnp.concatenate([weight_ref[pl.ds(me_d * col_per + h, 1), :] for h in range(col_per)], axis=1)
            scale = weight_own / jnp.maximum(size, 1.0)
        else:
            whole = jnp.dot(inverse, whole, precision=highest, preferred_element_type=F32)
        s.weighted[it, 0, 0] = (whole * scale).astype(BF16)

        def line_gather(kz):
            return remote(
                s.weighted.at[it, 0, 0], s.weighted.at[it, kz, 0], s.wt_send.at[it, kz, 0], s.wt_recv.at[it, kz, 0], to(2 * kz, 0)
            )

        def pair_gather(kz):
            return remote(
                s.weighted.at[it, kz, 0], s.weighted.at[it, kz, 1], s.wt_send.at[it, kz, 1], s.wt_recv.at[it, kz, 1], to(1, 0)
            )

        for kz in range(nz - 1, 0, -1):
            line_gather(kz).start()
        pair_gather(0).start()

        def source(kz, side):
            return flip(me_d, 2 * kz + side, d_bits)

        def line_relay():
            return remote(
                s.weighted.at[it, 0, 1], s.weighted.at[it, 1, 1], s.wt_send.at[it, 1, 1], s.wt_recv.at[it, 1, 1], to(2, 0)
            )

        def add_block(kz, side, fresh=False):
            for q in range(nb):
                term = image_of(q, s.weighted[it, kz, side], source(kz, side))
                s.image[q] = term if fresh else s.image[q] + term

        add_block(0, 0, True)
        pair_gather(0).wait_recv()
        line_relay().start()
        add_block(0, 1)
        line_gather(1).wait_recv()
        add_block(1, 0)

        @pl.loop(2, nz)
        def _(kz):
            line_gather(kz).wait_recv()
            pair_gather(kz).start()
            add_block(kz, 0)

        line_relay().wait_recv()
        add_block(1, 1)

        @pl.loop(2, nz - 1)
        def _(kz):
            pair_gather(kz).wait_recv()
            add_block(kz, 1)

        pair_gather(nz - 1).wait_recv()

        def finish(k, h):
            q = flip(me_b, k, b_bits)
            term = image_of(q, s.weighted[it, nz - 1, 1], source(nz - 1, 1), h * half_per, (h + 1) * half_per)
            return s.image[q, :, h * half_rows : (h + 1) * half_rows] + term

        def mate_copy(k, h):
            return remote(
                s.mate_out.at[it, k, h], s.mate_in.at[it, k, h], s.mate_send.at[it, k, h], s.mate_recv.at[it, k, h], to(0, 1)
            )

        def far_copy(h):
            return remote(s.far_out.at[it, h], s.far_in.at[it, h], s.far_send.at[it, h], s.far_recv.at[it, h], to(0, 2))

        def weigh(value, h):
            parts = [
                value[:, i * tile : (i + 1) * tile] * inv_own[h * half_per + i : h * half_per + i + 1]
                for i in range(half_per)
            ]
            return jnp.concatenate(parts, axis=1)

        for h in range(2):
            s.mate_out[it, 1, h] = finish(3, h).astype(BF16)
            mate_copy(1, h).start()
        for h in range(2):
            both = finish(2, h)
            mate_copy(1, h).wait_recv()
            s.far_out[it, h] = (both + s.mate_in[it, 1, h].astype(F32)).astype(BF16)
            far_copy(h).start()
        for h in range(2):
            s.mate_out[it, 0, h] = finish(1, h).astype(BF16)
            mate_copy(0, h).start()
        halves = [finish(0, h) for h in range(2)]
        more = it + 1 < ITERS
        for h in range(2):
            mate_copy(0, h).wait_recv()
            far_copy(h).wait_recv()
            halves[h] = weigh(halves[h] + s.mate_in[it, 0, h].astype(F32) + s.far_in[it, h].astype(F32), h)
            if more:
                s.band[it + 1, 0, h] = weigh(halves[h], h).astype(BF16)
                for k in (2, 1):
                    band_copy(k, h).start()
            gram = gram_part(halves[h]) if h == 0 else gram + gram_part(halves[h])
        image = jnp.concatenate(halves, axis=1)
        if more:
            gram_sent = gram_step(0, gram_of(gram))
        else:
            s.final[...] = image
            store = pltpu.make_async_copy(s.final, image_hbm, s.store_sem)
            store.start()
            gram_sent = gram_start(it, gram)
            waits += gram_sent
            gram_sent_two = gram_middle(it, gram_sent)
            waits += gram_sent_two
            gram = gram_end(it, gram_sent_two)
            inverse = inverse_factor(gram, k_vec)
            out_ref[...] = inverse
            store.wait()
        for h in range(2):
            for k in range(2):
                mate_copy(k, h).wait_send()
            far_copy(h).wait_send()
        for kz in range(nz):
            pair_copy(kz).wait_send()
            (line_relay() if kz == 1 else pair_gather(kz)).wait_send()
        for kz in range(1, nz):
            line_copy(kz).wait_send()
            line_gather(kz).wait_send()
    for copy in waits:
        copy.wait_send()
    for k in range(1, nb):
        for h in range(2):
            band_copy(k, h).wait_send()


def scratch_of(nd, nb, slots, tile, k_vec, own_rows, own_cols):
    dma = pltpu.SemaphoreType.DMA
    row_tiles, col_tiles = own_rows * nb // tile, own_cols * nd // tile
    nz = nd // 2
    fold = (k_vec // 2, 2 * k_vec)
    buffers = {
        "tiles": ((slots, tile, tile), I32),
        "bits": ((slots + 1, tile, tile), BF16),
        "turned": ((slots + 1, tile, tile), BF16),
        "size_terms": ((slots + 1, 8, tile), F32),
        "doc_terms": ((slots + 1, 8, tile), F32),
        "table": ((8, tile), I32),
        "weight_terms": ((2, col_tiles, 16, tile), BF16),
        "degree_own": ((row_tiles, tile), F32),
        "degree": ((nb, row_tiles, tile), F32),
        "inv": ((row_tiles, tile), F32),
        "size": ((nd, 1, own_cols), F32),
        "size_from": ((nd, 1, own_cols), F32),
        "raw": ((nb, k_vec, own_rows), BF16),
        "band": ((ITERS, nb, 2, k_vec, own_rows // 2), BF16),
        "panel": ((nd, k_vec, own_cols), F32),
        "pair_out": ((ITERS, nz, k_vec, own_cols), BF16),
        "pair_in": ((ITERS, nz, k_vec, own_cols), BF16),
        "line_out": ((ITERS, nz, k_vec, own_cols), BF16),
        "line_in": ((ITERS, nz, k_vec, own_cols), BF16),
        "weighted": ((ITERS, nz, 2, k_vec, own_cols), BF16),
        "image": ((nb, k_vec, own_rows), F32),
        "mate_out": ((ITERS, 2, 2, k_vec, own_rows // 2), BF16),
        "mate_in": ((ITERS, 2, 2, k_vec, own_rows // 2), BF16),
        "far_out": ((ITERS, 2, k_vec, own_rows // 2), BF16),
        "far_in": ((ITERS, 2, k_vec, own_rows // 2), BF16),
        "final": ((k_vec, own_rows), F32),
        "gram_out": ((3,) + fold, F32),
        "gram_in": ((3,) + fold, F32),
        "gram_one": ((ITERS, 2 * nb) + fold, F32),
        "gram_two": ((ITERS, nz) + fold, F32),
    }
    total = 0
    for shape, kind in buffers.values():
        count = jnp.dtype(kind).itemsize
        for extent in shape:
            count *= extent
        total += count
    scratch = {name: pltpu.VMEM(shape, kind) for name, (shape, kind) in buffers.items()}
    scratch["slot"] = pltpu.SMEM((8, tile), I32)
    sems = {"load_sem": (CHUNKS,)}
    for name, shape in {
        "raw": (nb,),
        "deg": (nb,),
        "size": (nd,),
        "band": (nb, 2),
        "pair": (ITERS, nz),
        "line": (ITERS, nz),
        "wt": (ITERS, nz, 2),
        "mate": (ITERS, 2, 2),
        "far": (ITERS, 2),
        "gs": (3,),
        "g1": (ITERS, 2 * nb),
        "g2": (ITERS, nz),
    }.items():
        sems[name + "_send"] = shape
        sems[name + "_recv"] = shape
    for name, shape in sems.items():
        scratch[name] = dma(shape)
    scratch["table_sem"] = dma
    scratch["store_sem"] = dma
    return scratch, total


VMEM_BYTES = 60000 * 1024


def body(start_vectors, bucket_weight, tile_count, tile_coords, patterns):
    nd, nb = lax.axis_size("doc"), lax.axis_size("bkt")
    slots, tile = patterns.shape[2], patterns.shape[3]
    k_vec, own_rows = start_vectors.shape
    band_cols = bucket_weight.shape[0]
    own_cols = band_cols // nd
    scratch, total = scratch_of(nd, nb, slots, tile, k_vec, own_rows, own_cols)
    fits = total + 4 * k_vec * own_rows * 4 < VMEM_BYTES
    powers = nd & (nd - 1) == 0 and nd >= 4 and nb == 4
    whole = band_cols == nd * own_cols and own_cols == 2 * tile and 2 * k_vec == tile
    table = own_rows % (2 * tile) == 0 and own_rows // tile * (band_cols // tile) == tile and own_rows // tile % 8 == 0
    if not (fits and powers and whole and table and slots % (CHUNKS * GROUP) == 0):
        return plain_body(start_vectors, bucket_weight, tile_count, tile_coords, patterns)
    smem = pl.BlockSpec(memory_space=pltpu.SMEM)
    vmem = pl.BlockSpec(memory_space=pltpu.VMEM)
    anywhere = pl.BlockSpec(memory_space=pl.ANY)
    coords = tile_coords.reshape(slots, 2).T
    inverse, image = pl.pallas_call(
        functools.partial(kernel, tuple(scratch), nd, nb),
        out_shape=[jax.ShapeDtypeStruct((k_vec, k_vec), F32), jax.ShapeDtypeStruct((k_vec, own_rows), F32)],
        in_specs=[smem, smem, vmem, vmem, vmem, anywhere],
        out_specs=[vmem, anywhere],
        scratch_shapes=list(scratch.values()),
        compiler_params=pltpu.CompilerParams(
            collective_id=0, has_side_effects=True, vmem_limit_bytes=VMEM_BYTES
        ),
        name="subspace",
    )(tile_count, coords, coords, start_vectors, bucket_weight.reshape(band_cols // tile, tile), patterns.reshape(slots, tile, tile))
    return jnp.dot(inverse, image, precision=lax.Precision.HIGH)


def solution(mesh):
    in_specs = (
        P(None, ("doc", "bkt")),
        P("bkt"),
        P("doc", "bkt"),
        P("doc", "bkt", None, None),
        P("doc", "bkt", None, None, None),
    )
    out_specs = P(None, ("doc", "bkt"))
    return jax.shard_map(body, mesh=mesh, in_specs=in_specs, out_specs=out_specs, check_vma=False)
```
